256 devices in a mesh: grp: 4 (over y), seq: 64 (over z, x, core).
Axes of the slice: x: 4, y: 4, z: 8, core: 2. Of those that a mesh axis runs over, the one named last changes fastest.
Arguments:
- queries: bfloat16 [8192, 64, 192], P('seq', 'grp'), may hold values from -6 to 6
- key_cache: bfloat16 [4, 65536, 192], P('grp', 'seq'), may hold values from -6 to 6
- group_value_cache: bfloat16 [4, 65536, 128], P('grp', 'seq'), may hold values from -6 to 6
- coarse_keys: bfloat16 [4, 4096, 192], P('grp', 'seq'), may hold values from -6 to 6
- coarse_values: bfloat16 [4, 4096, 128], P('grp', 'seq'), may hold values from -6 to 6
- hidden: bfloat16 [8192, 2560], P('seq'), may hold values from -6 to 6
- gate_weight: bfloat16 [4, 2560, 32], P('grp'), may hold values from -0.125 to 0.125
- out_weight: bfloat16 [8192, 2560], P('grp'), may hold values from -0.09375 to 0.09375
- selected: int32 [4, 64, 16], P('grp', 'seq'), may hold values from 0 to 1023, as said below
Outputs:
- layer_out: bfloat16 [8192, 2560], P('seq', 'grp')
The draws below stay inside these ranges and needn't reach their ends.
Inputs may be any that keep to these rules, and one draw needn't show every extreme that they name: selected[g, t] lists 16 distinct blocks of 64 positions for tile t of group g; the first is block 0; none starts after the tile's last query position; at most 1 of them lie within one index of seq's 1024 positions.
All inputs are finite; a program needn't handle non-finite values.
Results may differ from the reference program's by a relative error of at most 0.013.
Values may be sent and summed in bfloat16 or wider, within the bound.
No kernel may reach another device: no remote copies, remote signals or barrier semaphores. Data moves between devices by JAX's collectives and lax.ppermute only.
A program may use at most 128 MiB of HBM per device.

```python
import jax
import jax.numpy as jnp
from jax import lax

D = 2560
HEADS = 64
GROUPS = 4
DQK = 192
DV = 128
BLK = 64
SEL = 16
TILE = 128
CSTRIDE = 16
CLEN = 32
HG = 16
TILES = 64
NQ = 8192
CONTEXT = 65536
NC = 4096
BLK_DEV = 16
CAP = 1
N_SEQ = 64


def draw_queries(key, part):
    full_shape = (NQ, HEADS, DQK)
    return jnp.clip(jax.random.normal(jax.random.fold_in(key, 11), full_shape, jnp.float32), -6.0, 6.0).astype(jnp.bfloat16)


def draw_key_cache(key, part):
    full_shape = (GROUPS, CONTEXT, DQK)
    return jnp.clip(jax.random.normal(jax.random.fold_in(key, 21), full_shape, jnp.float32), -6.0, 6.0).astype(jnp.bfloat16)


def draw_coarse_keys(key, part):
    full_shape = (GROUPS, NC, DQK)
    return jnp.clip(jax.random.normal(jax.random.fold_in(key, 23), full_shape, jnp.float32), -6.0, 6.0).astype(jnp.bfloat16)


def draw_selected(key, part):
    tile_ids = jnp.arange(TILES, dtype=jnp.int32)
    last_block = (CONTEXT - NQ + (tile_ids + 1) * TILE - 1) // BLK
    last_owner = last_block // BLK_DEV
    owner_ids = jnp.arange(N_SEQ, dtype=jnp.int32)
    slot_ids = jnp.arange(CAP, dtype=jnp.int32)
    owned = jnp.where(owner_ids[None, :] < last_owner[:, None], BLK_DEV, jnp.where(owner_ids[None, :] == last_owner[:, None], last_block[:, None] - last_owner[:, None] * BLK_DEV + 1, 0))
    is_first = (owner_ids[None, :] == 0).astype(jnp.int32)
    usable = owned - is_first
    slot_limit = jnp.minimum(usable, CAP - is_first)
    open_slot = slot_ids[None, None, :] < slot_limit[:, :, None]
    latest_blocks = owner_ids[None, :] >= last_owner[:, None] - 1
    preferred_blocks = (owner_ids[None, :] <= 1) | (owner_ids[None, :] >= last_owner[:, None] - 6)
    preference_boost = jnp.where(latest_blocks, 2 ** 20, 0) + jnp.where(preferred_blocks, 2 ** 16, 0)
    random_noise = jax.random.randint(jax.random.fold_in(key, 31), (GROUPS, TILES, N_SEQ, CAP), 0, 2 ** 16)
    logit_scores = random_noise + preference_boost[None, :, :, None]
    flat_ids = owner_ids[:, None] * CAP + slot_ids[None, :]
    ranked = jnp.where(open_slot[None], logit_scores + 1, 0) * (N_SEQ * CAP) + flat_ids[None, None]
    ranked = ranked.reshape(GROUPS, TILES, N_SEQ * CAP)
    top_values, chosen = lax.top_k(ranked, SEL - 1)
    chosen_owner = chosen // CAP
    chosen_slot = chosen % CAP
    rotation = jax.random.randint(jax.random.fold_in(key, 37), (GROUPS, TILES, N_SEQ), 0, 2 ** 20)
    usable_all = jnp.broadcast_to(usable[None], (GROUPS, TILES, N_SEQ))
    block_span = jnp.maximum(jnp.take_along_axis(usable_all, chosen_owner, axis=2), 1)
    start_pick = jnp.take_along_axis(rotation, chosen_owner, axis=2) % block_span
    within = (start_pick + chosen_slot) % block_span + (chosen_owner == 0).astype(jnp.int32)
    blocks = chosen_owner * BLK_DEV + within
    sink_block = jnp.zeros((GROUPS, TILES, 1), jnp.int32)
    return jnp.concatenate([sink_block, blocks.astype(jnp.int32)], axis=2)


def spiked(drawn, key, source, target, shards_of, factor):
    def block_of(dim):
        return (jnp.arange(drawn.shape[dim]) // (drawn.shape[dim] // shards_of)).reshape((-1,) + (1,) * (drawn.ndim - 1 - dim))

    first = jax.random.permutation(key, shards_of)[block_of(target)]
    far = (block_of(target) + shards_of // 2) % shards_of
    return jnp.where((block_of(source) == first) | (block_of(source) == far), factor * drawn, drawn)


def shard_levels(rng, dims, cuts, smallest, high):
    level = 1.0
    for position, blocks in cuts:
        steps = jax.random.uniform(jax.random.fold_in(jax.random.fold_in(rng, 6), position), (blocks,), jnp.float32, smallest / len(cuts), high / len(cuts))
        level = level * jnp.repeat(jnp.exp(steps), dims[position] // blocks).reshape((-1,) + (1,) * (len(dims) - 1 - position))
    return level


def gaussian(key, shape, scale, most, shards=(), kind=jnp.bfloat16):
    entries = scale * jax.random.normal(key, shape, jnp.float32)
    if shards:
        entries = entries * shard_levels(key, shape, shards, -0.22, 0.18)
    return jnp.clip(entries, -most, most).astype(kind)


def gaussian_with(key, dims, scale, most, split, heavy, kind=jnp.bfloat16):
    drawn = scale * jax.random.normal(key, dims, jnp.float32)
    if split:
        drawn = drawn * shard_levels(key, dims, split, -0.22, 0.18)
    return jnp.clip(spiked(drawn, jax.random.fold_in(key, 3), *heavy), -most, most).astype(kind)


def setup_inputs(seed: int = 0) -> dict:
    streams_of = jax.random.split(jax.random.key(seed), 10)
    return {
        "queries": draw_queries(jax.random.fold_in(streams_of[9], 71), 0),
        "key_cache": draw_key_cache(jax.random.fold_in(streams_of[9], 71), 0),
        "group_value_cache": gaussian(streams_of[2], (GROUPS, CONTEXT, DV), 1.0, 6.0, ((0, 4), (1, 64))),
        "coarse_keys": draw_coarse_keys(jax.random.fold_in(streams_of[9], 71), 0),
        "coarse_values": gaussian(streams_of[4], (GROUPS, NC, DV), 1.0, 6.0, ((0, 4), (1, 64))),
        "hidden": gaussian(streams_of[5], (NQ, D), 1.0, 6.0, ((0, 64),)),
        "gate_weight": gaussian(streams_of[6], (GROUPS, D, 2 * HG), D ** -0.5, 0.125, ((0, 4),)),
        "out_weight": gaussian_with(streams_of[7], (HEADS * DV, D), (HEADS * DV) ** -0.5, 0.09375, ((0, 4),), (0, 1, 4, 2.0)),
        "selected": draw_selected(jax.random.fold_in(streams_of[9], 71), 0),
    }


def branch(query_rows, row_pos, key_rows, value_rows, key_pos):
    logit_scores = jnp.dot(query_rows, key_rows.T, preferred_element_type=jnp.float32) * (DQK ** -0.5)
    logit_scores = jnp.where(key_pos[None, :] <= row_pos[:, None], logit_scores, -jnp.inf)
    row_max = jnp.max(logit_scores, axis=1, keepdims=True)
    weights = jnp.exp(logit_scores - row_max)
    row_total = jnp.sum(weights, axis=1, keepdims=True)
    return jnp.dot(weights.astype(jnp.bfloat16), value_rows, preferred_element_type=jnp.float32) / row_total


def reference(queries, key_cache, group_value_cache, coarse_keys, coarse_values, hidden, gate_weight, out_weight, selected):
    coarse_pos = jnp.arange(NC, dtype=jnp.int32) * CSTRIDE + CLEN - 1
    offsets = jnp.arange(BLK, dtype=jnp.int32)

    def one_tile(flat_index):
        group_index = (flat_index // TILES).astype(jnp.int32)
        tile_index = (flat_index % TILES).astype(jnp.int32)
        first_row = (tile_index * TILE).astype(jnp.int32)
        query_rows = lax.dynamic_slice(queries, (first_row, (group_index * HG).astype(jnp.int32), jnp.int32(0)), (TILE, HG, DQK)).reshape(TILE * HG, DQK)
        query_pos = (CONTEXT - NQ + first_row + jnp.arange(TILE, dtype=jnp.int32)).astype(jnp.int32)
        row_pos = jnp.repeat(query_pos, HG)
        group_keys = lax.dynamic_index_in_dim(key_cache, group_index, 0, keepdims=False)
        group_values = lax.dynamic_index_in_dim(group_value_cache, group_index, 0, keepdims=False)
        coarse_k = lax.dynamic_index_in_dim(coarse_keys, group_index, 0, keepdims=False)
        coarse_v = lax.dynamic_index_in_dim(coarse_values, group_index, 0, keepdims=False)
        coarse = branch(query_rows, row_pos, coarse_k, coarse_v, coarse_pos)
        group_sel = lax.dynamic_index_in_dim(selected, group_index, 0, keepdims=False)
        blocks = lax.dynamic_index_in_dim(group_sel, tile_index, 0, keepdims=False)
        key_pos = (blocks[:, None] * BLK + offsets[None, :]).reshape(-1).astype(jnp.int32)
        picked_block_index = branch(query_rows, row_pos, group_keys[key_pos], group_values[key_pos], key_pos)
        tile_hidden = lax.dynamic_slice_in_dim(hidden, first_row, TILE, 0)
        group_gate = lax.dynamic_index_in_dim(gate_weight, group_index, 0, keepdims=False)
        gate_logits = jnp.dot(tile_hidden, group_gate, preferred_element_type=jnp.float32)
        gate_coarse = jax.nn.sigmoid(gate_logits[:, :HG])
        gate_picked = jax.nn.sigmoid(gate_logits[:, HG:])
        mixed_heads = gate_coarse[:, :, None] * coarse.reshape(TILE, HG, DV) + gate_picked[:, :, None] * picked_block_index.reshape(TILE, HG, DV)
        return mixed_heads.astype(jnp.bfloat16).reshape(TILE, HG * DV)

    tiles_out = lax.map(one_tile, jnp.arange(GROUPS * TILES, dtype=jnp.int32))
    attended = tiles_out.reshape(GROUPS, TILES, TILE, HG * DV).transpose(1, 2, 0, 3).reshape(NQ, HEADS * DV)
    return jnp.dot(attended, out_weight, preferred_element_type=jnp.float32).astype(jnp.bfloat16)
```

```python
import functools
import math

import jax
import jax.numpy as jnp
from jax import lax
from jax.experimental import pallas as pl
from jax.experimental.pallas import tpu as pltpu
from jax.sharding import PartitionSpec as P

BLK = 64
SEL = 16
TILE = 128
CSTRIDE = 16
CLEN = 32
DQK = 192
DV = 128
PACK = BLK + BLK + BLK // 2
NEGATIVE = -1e30
EXP_SCALE = DQK**-0.5 * math.log2(math.e)
Z, X, C = 8, 4, 2


def packed_blocks(keys, values):
    high = jnp.concatenate([keys[:, : BLK // 2, DV:], keys[:, BLK // 2 :, DV:]], axis=2)
    return jnp.concatenate([keys[:, :, :DV], values, high], axis=1)


def unpacked_keys(block):
    high = jnp.concatenate([block[2 * BLK :, :BLK], block[2 * BLK :, BLK:]], axis=0)
    return jnp.concatenate([block[:BLK], high], axis=1)


def copies_for(x, groups):
    peers = len(groups[0])
    return lax.all_to_all(
        jnp.broadcast_to(x[None], (peers, *x.shape)), "seq", 0, 0, axis_index_groups=groups, tiled=True
    )


def everywhere(block):
    along_z = [[(z * X + x) * C + c for z in range(Z)] for x in range(X) for c in range(C)]
    along_x = [[(z * X + x) * C + c for x in range(X)] for z in range(Z) for c in range(C)]
    along_c = [[(z * X + x) * C + c for c in range(C)] for z in range(Z) for x in range(X)]
    block = copies_for(block, along_z)
    block = copies_for(block, along_x)
    return copies_for(block, along_c).reshape(C * X * Z, PACK, DV)


def payload_kernel(wanted_ref, blocks_ref, out_ref):
    def one(t, carry):
        out_ref[t] = blocks_ref[wanted_ref[t]]
        return carry

    lax.fori_loop(0, out_ref.shape[0], one, 0, unroll=8)


def payload(wanted, blocks):
    tiles = wanted.shape[0]
    whole = lambda shape: pl.BlockSpec(shape, lambda i, w: (0, 0, 0))
    return pl.pallas_call(
        payload_kernel,
        grid_spec=pltpu.PrefetchScalarGridSpec(
            num_scalar_prefetch=1,
            grid=(1,),
            in_specs=[whole(blocks.shape)],
            out_specs=whole((tiles, PACK, DV)),
        ),
        out_shape=jax.ShapeDtypeStruct((tiles, PACK, DV), blocks.dtype),
        cost_estimate=pl.CostEstimate(flops=0, bytes_accessed=2 * tiles * PACK * DV * 2, transcendentals=0),
        compiler_params=pltpu.CompilerParams(vmem_limit_bytes=16 << 20),
        name="payload",
    )(wanted, blocks)


def coarse_kernel(info_ref, kv_ref, q_ref, gate_ref, out_ref, keys, values_t, scores):
    n_chunks = C * X
    rows = Z * BLK

    @pl.when(pl.program_id(0) == 0)
    def _():
        def one(n, carry):
            at = pl.multiple_of(n * 2 * BLK, 2 * BLK)
            keys[pl.ds(at, BLK), :] = unpacked_keys(kv_ref[2 * n])
            keys[pl.ds(at + BLK, BLK), :] = unpacked_keys(kv_ref[2 * n + 1])
            v = jnp.concatenate([kv_ref[2 * n, BLK : 2 * BLK], kv_ref[2 * n + 1, BLK : 2 * BLK]], axis=0)
            values_t[:, pl.ds(at, 2 * BLK)] = v.T
            return carry

        lax.fori_loop(0, n_chunks * Z // 2, one, 0)

    q = jnp.concatenate([q_ref[0], q_ref[1]], axis=1)
    width = q.shape[1]
    late = 2 * BLK
    row = lax.broadcasted_iota(jnp.int32, (late, width), 0)
    lane = lax.broadcasted_iota(jnp.int32, (late, width), 1)
    z = Z - 2 + row // BLK
    token0 = z * (X * C * BLK) + row % BLK
    query_pos = info_ref[0] + lane % TILE
    top = jnp.full((1, width), NEGATIVE, jnp.float32)
    for n in range(n_chunks):
        c, x = divmod(n, X)
        s = jnp.dot(keys[n * rows : (n + 1) * rows, :], q, preferred_element_type=jnp.float32)
        token = token0 + (x * C + c) * BLK
        tail = jnp.where(token * CSTRIDE + CLEN - 1 <= query_pos, s[rows - late :], NEGATIVE)
        scores[n * rows : (n + 1) * rows - late, :] = s[: rows - late]
        scores[(n + 1) * rows - late : (n + 1) * rows, :] = tail
        top = jnp.maximum(top, jnp.max(s[: rows - late], axis=0, keepdims=True))
        top = jnp.maximum(top, jnp.max(tail, axis=0, keepdims=True))
    total = jnp.zeros((1, width), jnp.float32)
    acc = jnp.zeros((DV, width), jnp.float32)
    for n in range(n_chunks):
        w = jnp.exp2((scores[n * rows : (n + 1) * rows, :] - top) * EXP_SCALE)
        total = total + jnp.sum(w, axis=0, keepdims=True)
        acc = acc + jnp.dot(
            values_t[:, n * rows : (n + 1) * rows], w.astype(jnp.bfloat16), preferred_element_type=jnp.float32
        )
    gate = jnp.concatenate([gate_ref[0], gate_ref[1]], axis=1)
    acc = acc * (gate / total)
    out_ref[0] = acc[:, :TILE]
    out_ref[1] = acc[:, TILE:]


def coarse_branch(info, coarse, queries_t, gate):
    heads = queries_t.shape[0]
    tokens = coarse.shape[0] * BLK
    pair = lambda shape: pl.BlockSpec((2, *shape), lambda p, i: (p, 0, 0))
    return pl.pallas_call(
        coarse_kernel,
        grid_spec=pltpu.PrefetchScalarGridSpec(
            num_scalar_prefetch=1,
            grid=(heads // 2,),
            in_specs=[
                pl.BlockSpec(coarse.shape, lambda p, i: (0, 0, 0), pipeline_mode=pl.Buffered(1)),
                pair((DQK, TILE)),
                pair((1, TILE)),
            ],
            out_specs=pair((DV, TILE)),
            scratch_shapes=[
                pltpu.VMEM((tokens, DQK), jnp.bfloat16),
                pltpu.VMEM((DV, tokens), jnp.bfloat16),
                pltpu.VMEM((tokens, 2 * TILE), jnp.float32),
            ],
        ),
        out_shape=jax.ShapeDtypeStruct((heads, DV, TILE), jnp.float32),
        cost_estimate=pl.CostEstimate(
            flops=2 * heads * TILE * tokens * (DQK + DV),
            bytes_accessed=tokens * (DQK + DV) * 2 + heads * TILE * (DQK * 2 + DV * 4),
            transcendentals=heads * TILE * tokens,
        ),
        compiler_params=pltpu.CompilerParams(vmem_limit_bytes=24 << 20),
        name="coarse",
    )(info, coarse, queries_t, gate)


def tail_kernel(
    n_grp, info_ref, incoming_ref, q_ref, gate_ref, coarse_ref, weight_ref, *rest
):
    outs, (blocks, keys, values_t, scores, attended, weight, block_sem, weight_sem) = rest[:n_grp], rest[n_grp:]
    heads = q_ref.shape[0]
    cols = weight.shape[2]
    base, grp = info_ref[0], info_ref[1]
    late = SEL - 1
    for j in range(SEL):
        late = jnp.where(info_ref[2 + j] * BLK >= base, j, late)
    copies = []
    for j in range(SEL):
        slot_from = jnp.where(late == j, SEL - 1, j) if j < SEL - 1 else late
        owner = info_ref[2 + slot_from] // (1024 // BLK)
        copies.append(pltpu.make_async_copy(incoming_ref.at[owner], blocks.at[j], block_sem.at[j]))
    for copy in copies:
        copy.start()
    weight_copies = []
    for k in range(n_grp):
        at = pl.multiple_of(lax.rem(grp + k, n_grp) * cols, DV)
        weight_copies.append(
            pltpu.make_async_copy(weight_ref.at[:, pl.ds(at, cols)], weight.at[k], weight_sem.at[k])
        )
    for copy in weight_copies:
        copy.start()
    for j in range(0, SEL, 2):
        copies[j].wait()
        copies[j + 1].wait()
        keys[j * BLK : (j + 1) * BLK, :] = unpacked_keys(blocks[j])
        keys[(j + 1) * BLK : (j + 2) * BLK, :] = unpacked_keys(blocks[j + 1])
        v = jnp.concatenate([blocks[j, BLK : 2 * BLK], blocks[j + 1, BLK : 2 * BLK]], axis=0)
        values_t[:, j * BLK : (j + 2) * BLK] = v.T
    width = 2 * TILE
    n_keys = SEL * BLK
    row = lax.broadcasted_iota(jnp.int32, (BLK, width), 0)
    lane = lax.broadcasted_iota(jnp.int32, (BLK, width), 1)
    seen = info_ref[2 + late] * BLK + row <= base + lane % TILE

    for p in range(heads // 2):
        q = jnp.concatenate([q_ref[2 * p], q_ref[2 * p + 1]], axis=1)
        s = jnp.dot(keys[...], q, preferred_element_type=jnp.float32)
        last = jnp.where(seen, s[n_keys - BLK :], NEGATIVE)
        top = jnp.maximum(
            jnp.max(s[: n_keys - BLK], axis=0, keepdims=True), jnp.max(last, axis=0, keepdims=True)
        )
        w = jnp.exp2((jnp.concatenate([s[: n_keys - BLK], last], axis=0) - top) * EXP_SCALE)
        total = jnp.sum(w, axis=0, keepdims=True)
        o = jnp.dot(values_t[...], w.astype(jnp.bfloat16), preferred_element_type=jnp.float32)
        gate = jnp.concatenate([gate_ref[2 * p], gate_ref[2 * p + 1]], axis=1)
        o = o * (gate / total)
        for i in range(2):
            h = 2 * p + i
            both = o[:, i * TILE : (i + 1) * TILE] + coarse_ref[h]
            attended[:, h * DV : (h + 1) * DV] = both.T.astype(jnp.bfloat16)
    for k in range(n_grp):
        weight_copies[k].wait()
    for k in range(n_grp):
        part = jnp.dot(attended[...], weight[k], preferred_element_type=jnp.float32)
        outs[k][...] = part.astype(outs[k].dtype)


def tail(info, incoming, queries_t, gate, coarse_out, out_weight, n_grp):
    heads = queries_t.shape[0]
    rows, model = out_weight.shape
    cols = model // n_grp
    vmem = lambda shape: pl.BlockSpec(shape, lambda i, s: (0,) * len(shape))
    anywhere = pl.BlockSpec(memory_space=pl.ANY)
    return pl.pallas_call(
        functools.partial(tail_kernel, n_grp),
        grid_spec=pltpu.PrefetchScalarGridSpec(
            num_scalar_prefetch=1,
            grid=(1,),
            in_specs=[
                anywhere,
                vmem(queries_t.shape),
                vmem(gate.shape),
                vmem(coarse_out.shape),
                anywhere,
            ],
            out_specs=[vmem((TILE, cols))] * n_grp,
            scratch_shapes=[
                pltpu.VMEM((SEL, PACK, DV), jnp.bfloat16),
                pltpu.VMEM((SEL * BLK, DQK), jnp.bfloat16),
                pltpu.VMEM((DV, SEL * BLK), jnp.bfloat16),
                pltpu.VMEM((SEL * BLK, 2 * TILE), jnp.float32),
                pltpu.VMEM((TILE, rows), jnp.bfloat16),
                pltpu.VMEM((n_grp, rows, cols), jnp.bfloat16),
                pltpu.SemaphoreType.DMA((SEL,)),
                pltpu.SemaphoreType.DMA((n_grp,)),
            ],
        ),
        out_shape=[jax.ShapeDtypeStruct((TILE, cols), jnp.float32)]
        + [jax.ShapeDtypeStruct((TILE, cols), jnp.bfloat16)] * (n_grp - 1),
        cost_estimate=pl.CostEstimate(
            flops=2 * heads * TILE * SEL * BLK * (DQK + DV) + 2 * TILE * rows * model,
            bytes_accessed=rows * model * 2,
            transcendentals=heads * TILE * SEL * BLK,
        ),
        compiler_params=pltpu.CompilerParams(vmem_limit_bytes=40 << 20),
        name="tail",
    )(info, incoming, queries_t, gate, coarse_out, out_weight)


def shards(
    queries,
    key_cache,
    group_value_cache,
    coarse_keys,
    coarse_values,
    hidden,
    gate_weight,
    out_weight,
    selected,
):
    seq_count = lax.axis_size("seq")
    n_grp = lax.axis_size("grp")
    seq_index = lax.axis_index("seq")
    grp_index = lax.axis_index("grp")
    ctx_dev = key_cache.shape[1]
    context = ctx_dev * seq_count
    heads = queries.shape[1]
    blocks_dev = ctx_dev // BLK

    own_list = selected[0, 0]
    owners = jnp.arange(seq_count, dtype=jnp.int32)
    mine = (own_list[None, :] // blocks_dev == owners[:, None]).astype(jnp.int32)
    wanted = jnp.sum(mine * (own_list % blocks_dev)[None, :], axis=1)
    wanted = jnp.broadcast_to(wanted[:, None, None], (seq_count, 1, SEL))
    wanted = lax.all_to_all(wanted, "seq", 0, 0, tiled=True)[:, 0, 0]

    blocks = packed_blocks(
        key_cache[0].reshape(blocks_dev, BLK, DQK), group_value_cache[0].reshape(blocks_dev, BLK, DV)
    )
    incoming = lax.all_to_all(payload(wanted, blocks), "seq", 0, 0, tiled=True)

    coarse = everywhere(packed_blocks(coarse_keys, coarse_values))

    first_pos = context - TILE * seq_count + seq_index * TILE
    info = jnp.concatenate([jnp.stack([first_pos, grp_index]).astype(jnp.int32), own_list])
    queries_t = jnp.transpose(queries, (1, 2, 0))
    gates = jax.nn.sigmoid(
        lax.dot_general(
            gate_weight[0], hidden, (((0,), (1,)), ((), ())), preferred_element_type=jnp.float32
        )
    )[:, None, :]
    coarse_out = coarse_branch(info, coarse, queries_t, gates[:heads])
    own, *others = tail(info, incoming, queries_t, gates[heads:], coarse_out, out_weight, n_grp)
    for k, part in enumerate(others, 1):
        perm = [(i, (i + k) % n_grp) for i in range(n_grp)]
        own = own + lax.ppermute(part, "grp", perm).astype(jnp.float32)
    return own.astype(jnp.bfloat16)


def solution(mesh):
    return jax.shard_map(
        shards,
        mesh=mesh,
        in_specs=(
            P("seq", "grp", None),
            P("grp", "seq", None),
            P("grp", "seq", None),
            P("grp", "seq", None),
            P("grp", "seq", None),
            P("seq", None),
            P("grp", None, None),
            P("grp", None),
            P("grp", "seq", None),
        ),
        out_specs=P("seq", "grp"),
        check_vma=False,
    )
```

```python
import functools
import math

import jax
import jax.numpy as jnp
from jax import lax
from jax.experimental import pallas as pl
from jax.experimental.pallas import tpu as pltpu
from jax.sharding import PartitionSpec as P

BLK = 64
SEL = 16
TILE = 128
CSTRIDE = 16
CLEN = 32
DQK = 192
DV = 128
PACK = BLK + BLK + BLK // 2
NEGATIVE = -1e30
EXP_SCALE = DQK**-0.5 * math.log2(math.e)
Z, X, C = 8, 4, 2


def packed_blocks(keys, values):
    high = jnp.concatenate([keys[:, : BLK // 2, DV:], keys[:, BLK // 2 :, DV:]], axis=2)
    return jnp.concatenate([keys[:, :, :DV], values, high], axis=1)


def unpacked_keys(block):
    high = jnp.concatenate([block[2 * BLK :, :BLK], block[2 * BLK :, BLK:]], axis=0)
    return jnp.concatenate([block[:BLK], high], axis=1)


def shifted(x, step):
    index = lambda z, x, c: ((z % Z) * X + x % X) * C + c % C
    dz, dx, dc = step
    perm = [(index(z, x, c), index(z + dz, x + dx, c + dc)) for z in range(Z) for x in range(X) for c in range(C)]
    return lax.ppermute(x, "seq", perm)


def everywhere(block, after):
    columns = jnp.concatenate([block] + [shifted(block, (k, 0, 0)) for k in range(1, Z)], axis=0)
    columns, _ = lax.optimization_barrier((columns, after))
    near = [columns] + [shifted(columns, (0, k, 0)) for k in range(1, X)]
    return near + [shifted(part, (0, 0, 1)) for part in near]


def payload_kernel(wanted_ref, blocks_ref, out_ref):
    def one(t, carry):
        out_ref[t] = blocks_ref[wanted_ref[t, 0, 0]]
        return carry

    lax.fori_loop(0, out_ref.shape[0], one, 0, unroll=8)


def payload(wanted, blocks):
    tiles = wanted.shape[0]
    whole = lambda shape: pl.BlockSpec(shape, lambda i, w: (0, 0, 0))
    return pl.pallas_call(
        payload_kernel,
        grid_spec=pltpu.PrefetchScalarGridSpec(
            num_scalar_prefetch=1,
            grid=(1,),
            in_specs=[whole(blocks.shape)],
            out_specs=whole((tiles, PACK, DV)),
        ),
        out_shape=jax.ShapeDtypeStruct((tiles, PACK, DV), blocks.dtype),
        cost_estimate=pl.CostEstimate(flops=0, bytes_accessed=2 * tiles * PACK * DV * 2, transcendentals=0),
        compiler_params=pltpu.CompilerParams(vmem_limit_bytes=16 << 20),
        name="payload",
    )(wanted, blocks)


def coarse_kernel(first_late, info_ref, *rest):
    kv_refs, (q_ref, gate_ref, out_ref, keys, values_t, scores) = rest[: C * X], rest[C * X :]
    n_tokens = keys.shape[0]

    @pl.when(pl.program_id(0) == 0)
    def _():
        me = info_ref[2]
        my_c, my_x, my_z = me % C, me // C % X, me // (C * X)

        def one(dx, x, dz, swapped):
            z = (my_z + Z - dz) % Z
            at = pl.multiple_of((z * X + x) * (C * BLK), C * BLK)
            first = kv_refs[swapped * X + dx].at[dz]
            second = kv_refs[(1 - swapped) * X + dx].at[dz]
            keys[pl.ds(at, BLK), :] = unpacked_keys(first)
            keys[pl.ds(at + BLK, BLK), :] = unpacked_keys(second)
            v = jnp.concatenate([first[BLK : 2 * BLK], second[BLK : 2 * BLK]], axis=0)
            values_t[:, pl.ds(at, C * BLK)] = v.T

        for swapped in range(C):

            @pl.when(my_c == swapped)
            def _(swapped=swapped):
                for dx in range(X):
                    x = (my_x + X - dx) % X

                    def step(dz, carry, dx=dx, x=x):
                        one(dx, x, dz, swapped)
                        return carry

                    lax.fori_loop(0, Z, step, 0)

    q = jnp.concatenate([q_ref[0], q_ref[1]], axis=1)
    width = q.shape[1]
    rows = 512
    row = lax.broadcasted_iota(jnp.int32, (rows, width), 0)
    query_pos = info_ref[0] + lax.broadcasted_iota(jnp.int32, (rows, width), 1) % TILE
    top = jnp.full((1, width), NEGATIVE, jnp.float32)
    for at in range(0, n_tokens, rows):
        s = jnp.dot(keys[at : at + rows, :], q, preferred_element_type=jnp.float32)
        if at + rows > first_late:
            s = jnp.where((at + row) * CSTRIDE + CLEN - 1 <= query_pos, s, NEGATIVE)
        scores[at : at + rows, :] = s
        top = jnp.maximum(top, jnp.max(s, axis=0, keepdims=True))
    total = jnp.zeros((1, width), jnp.float32)
    acc = jnp.zeros((DV, width), jnp.float32)
    for at in range(0, n_tokens, rows):
        w = jnp.exp2((scores[at : at + rows, :] - top) * EXP_SCALE)
        total = total + jnp.sum(w, axis=0, keepdims=True)
        acc = acc + jnp.dot(
            values_t[:, at : at + rows], w.astype(jnp.bfloat16), preferred_element_type=jnp.float32
        )
    gate = jnp.concatenate([gate_ref[0], gate_ref[1]], axis=1)
    acc = acc * (gate / total)
    out_ref[0] = acc[:, :TILE]
    out_ref[1] = acc[:, TILE:]


def coarse_branch(info, coarse, queries_t, gate, first_query):
    heads = queries_t.shape[0]
    tokens = C * X * Z * BLK
    pair = lambda shape: pl.BlockSpec((2, *shape), lambda p, i: (p, 0, 0))
    return pl.pallas_call(
        functools.partial(coarse_kernel, (first_query - CLEN + 1) // CSTRIDE + 1),
        grid_spec=pltpu.PrefetchScalarGridSpec(
            num_scalar_prefetch=1,
            grid=(heads // 2,),
            in_specs=[
                *[pl.BlockSpec(part.shape, lambda p, i: (0, 0, 0), pipeline_mode=pl.Buffered(1)) for part in coarse],
                pair((DQK, TILE)),
                pair((1, TILE)),
            ],
            out_specs=pair((DV, TILE)),
            scratch_shapes=[
                pltpu.VMEM((tokens, DQK), jnp.bfloat16),
                pltpu.VMEM((DV, tokens), jnp.bfloat16),
                pltpu.VMEM((tokens, 2 * TILE), jnp.float32),
            ],
        ),
        out_shape=jax.ShapeDtypeStruct((heads, DV, TILE), jnp.float32),
        cost_estimate=pl.CostEstimate(
            flops=2 * heads * TILE * tokens * (DQK + DV),
            bytes_accessed=tokens * (DQK + DV) * 2 + heads * TILE * (DQK * 2 + DV * 4),
            transcendentals=heads * TILE * tokens,
        ),
        compiler_params=pltpu.CompilerParams(vmem_limit_bytes=24 << 20),
        name="coarse",
    )(info, *coarse, queries_t, gate)


def tail_kernel(
    n_grp, info_ref, incoming_ref, q_ref, gate_ref, coarse_ref, weight_ref, *rest
):
    outs, scratch = rest[:n_grp], rest[n_grp:]
    blocks, keys, values_t, queries, coarse, attended, weight, block_sem, in_sem, weight_sem = scratch
    heads = q_ref.shape[0]
    cols = weight.shape[2]
    base, grp = info_ref[0], info_ref[1]
    late = SEL - 1
    for j in range(SEL):
        late = jnp.where(info_ref[3 + j] * BLK >= base, j, late)
    copies = []
    for j in range(SEL):
        slot_from = jnp.where(late == j, SEL - 1, j) if j < SEL - 1 else late
        owner = info_ref[3 + slot_from] // (1024 // BLK)
        copies.append(pltpu.make_async_copy(incoming_ref.at[owner], blocks.at[j], block_sem.at[j]))
    copies.append(pltpu.make_async_copy(q_ref, queries, in_sem.at[0]))
    copies.append(pltpu.make_async_copy(coarse_ref, coarse, in_sem.at[1]))
    for copy in copies:
        copy.start()
    weight_copies = []
    for k in range(n_grp):
        at = pl.multiple_of(lax.rem(grp + k, n_grp) * cols, DV)
        weight_copies.append(
            pltpu.make_async_copy(weight_ref.at[:, pl.ds(at, cols)], weight.at[k], weight_sem.at[k])
        )
    for copy in weight_copies:
        copy.start()
    for j in range(0, SEL, 2):
        copies[j].wait()
        copies[j + 1].wait()
        keys[j * BLK : (j + 1) * BLK, :] = unpacked_keys(blocks[j])
        keys[(j + 1) * BLK : (j + 2) * BLK, :] = unpacked_keys(blocks[j + 1])
        v = jnp.concatenate([blocks[j, BLK : 2 * BLK], blocks[j + 1, BLK : 2 * BLK]], axis=0)
        values_t[:, j * BLK : (j + 2) * BLK] = v.T
    copies[SEL].wait()
    copies[SEL + 1].wait()
    width = 2 * TILE
    n_keys = SEL * BLK
    row = lax.broadcasted_iota(jnp.int32, (BLK, width), 0)
    lane = lax.broadcasted_iota(jnp.int32, (BLK, width), 1)
    seen = info_ref[3 + late] * BLK + row <= base + lane % TILE

    for p in range(heads // 2):
        q = jnp.concatenate([queries[2 * p], queries[2 * p + 1]], axis=1)
        s = jnp.dot(keys[...], q, preferred_element_type=jnp.float32)
        last = jnp.where(seen, s[n_keys - BLK :], NEGATIVE)
        top = jnp.maximum(
            jnp.max(s[: n_keys - BLK], axis=0, keepdims=True), jnp.max(last, axis=0, keepdims=True)
        )
        w = jnp.exp2((jnp.concatenate([s[: n_keys - BLK], last], axis=0) - top) * EXP_SCALE)
        total = jnp.sum(w, axis=0, keepdims=True)
        o = jnp.dot(values_t[...], w.astype(jnp.bfloat16), preferred_element_type=jnp.float32)
        gate = jnp.concatenate([gate_ref[2 * p], gate_ref[2 * p + 1]], axis=1)
        o = o * (gate / total)
        for i in range(2):
            h = 2 * p + i
            both = o[:, i * TILE : (i + 1) * TILE] + coarse[h]
            attended[:, h * DV : (h + 1) * DV] = both.T.astype(jnp.bfloat16)
    for k in range(n_grp):
        weight_copies[k].wait()
    for k in range(n_grp):
        part = jnp.dot(attended[...], weight[k], preferred_element_type=jnp.float32)
        outs[k][...] = part.astype(outs[k].dtype)


def in_hbm(x):
    return pltpu.with_memory_space_constraint(x, pltpu.HBM)


def tail(info, incoming, queries_t, gate, coarse_out, out_weight, n_grp):
    heads = queries_t.shape[0]
    rows, model = out_weight.shape
    cols = model // n_grp
    vmem = lambda shape: pl.BlockSpec(shape, lambda i, s: (0,) * len(shape))
    hbm = pl.BlockSpec(memory_space=pltpu.HBM)
    return pl.pallas_call(
        functools.partial(tail_kernel, n_grp),
        grid_spec=pltpu.PrefetchScalarGridSpec(
            num_scalar_prefetch=1,
            grid=(1,),
            in_specs=[
                pl.BlockSpec(memory_space=pl.ANY),
                hbm,
                vmem(gate.shape),
                hbm,
                hbm,
            ],
            out_specs=[vmem((TILE, cols))] * n_grp,
            scratch_shapes=[
                pltpu.VMEM((SEL, PACK, DV), jnp.bfloat16),
                pltpu.VMEM((SEL * BLK, DQK), jnp.bfloat16),
                pltpu.VMEM((DV, SEL * BLK), jnp.bfloat16),
                pltpu.VMEM(queries_t.shape, queries_t.dtype),
                pltpu.VMEM(coarse_out.shape, coarse_out.dtype),
                pltpu.VMEM((TILE, rows), jnp.bfloat16),
                pltpu.VMEM((n_grp, rows, cols), jnp.bfloat16),
                pltpu.SemaphoreType.DMA((SEL,)),
                pltpu.SemaphoreType.DMA((2,)),
                pltpu.SemaphoreType.DMA((n_grp,)),
            ],
        ),
        out_shape=[jax.ShapeDtypeStruct((TILE, cols), jnp.float32)]
        + [jax.ShapeDtypeStruct((TILE, cols), jnp.bfloat16)] * (n_grp - 1),
        cost_estimate=pl.CostEstimate(
            flops=2 * heads * TILE * SEL * BLK * (DQK + DV) + 2 * TILE * rows * model,
            bytes_accessed=rows * model * 2,
            transcendentals=heads * TILE * SEL * BLK,
        ),
        compiler_params=pltpu.CompilerParams(vmem_limit_bytes=24 << 20),
        name="tail",
    )(info, incoming, in_hbm(queries_t), gate, in_hbm(coarse_out), in_hbm(out_weight))


def shards(
    queries,
    key_cache,
    group_value_cache,
    coarse_keys,
    coarse_values,
    hidden,
    gate_weight,
    out_weight,
    selected,
):
    seq_count = lax.axis_size("seq")
    n_grp = lax.axis_size("grp")
    seq_index = lax.axis_index("seq")
    grp_index = lax.axis_index("grp")
    ctx_dev = key_cache.shape[1]
    context = ctx_dev * seq_count
    heads = queries.shape[1]
    blocks_dev = ctx_dev // BLK

    own_list = selected[0, 0]
    owners = jnp.arange(seq_count, dtype=jnp.int32)
    mine = (own_list[None, :] // blocks_dev == owners[:, None]).astype(jnp.int32)
    wanted = jnp.sum(mine * (own_list % blocks_dev)[None, :], axis=1)
    wanted = lax.all_to_all(wanted[:, None, None], "seq", 0, 0, tiled=True)

    blocks = packed_blocks(
        key_cache[0].reshape(blocks_dev, BLK, DQK), group_value_cache[0].reshape(blocks_dev, BLK, DV)
    )
    outgoing = payload(wanted, blocks)
    coarse = everywhere(packed_blocks(coarse_keys, coarse_values), outgoing)
    incoming = lax.all_to_all(outgoing, "seq", 0, 0, tiled=True)

    first_query = context - TILE * seq_count
    first_pos = first_query + seq_index * TILE
    info = jnp.concatenate([jnp.stack([first_pos, grp_index, seq_index]).astype(jnp.int32), own_list])
    queries_t = jnp.transpose(queries, (1, 2, 0))
    gates = jax.nn.sigmoid(
        lax.dot_general(
            gate_weight[0], hidden, (((0,), (1,)), ((), ())), preferred_element_type=jnp.float32
        )
    )[:, None, :]
    coarse_out = coarse_branch(info, coarse, queries_t, gates[:heads], first_query)
    own, *others = tail(info, incoming, queries_t, gates[heads:], coarse_out, out_weight, n_grp)
    for k, part in enumerate(others, 1):
        perm = [(i, (i + k) % n_grp) for i in range(n_grp)]
        own = own + lax.ppermute(part, "grp", perm).astype(jnp.float32)
    return own.astype(jnp.bfloat16)


def solution(mesh):
    return jax.shard_map(
        shards,
        mesh=mesh,
        in_specs=(
            P("seq", "grp", None),
            P("grp", "seq", None),
            P("grp", "seq", None),
            P("grp", "seq", None),
            P("grp", "seq", None),
            P("seq", None),
            P("grp", None, None),
            P("grp", None),
            P("grp", "seq", None),
        ),
        out_specs=P("seq", "grp"),
        check_vma=False,
    )
```

```python
import functools
import math

import jax
import jax.numpy as jnp
from jax import lax
from jax.experimental import pallas as pl
from jax.experimental.pallas import tpu as pltpu
from jax.sharding import PartitionSpec as P

BLK = 64
SEL = 16
TILE = 128
CSTRIDE = 16
CLEN = 32
DQK = 192
DV = 128
PACK = BLK + BLK + BLK // 2
PADDED = 512
NEGATIVE = -1e30
EXP_SCALE = DQK**-0.5 * math.log2(math.e)
Z, X, C = 8, 4, 2


def packed_blocks(keys, values):
    high = jnp.concatenate([keys[:, : BLK // 2, DV:], keys[:, BLK // 2 :, DV:]], axis=2)
    return jnp.concatenate([keys[:, :, :DV], values, high], axis=1)


def unpacked_keys(block):
    high = jnp.concatenate([block[2 * BLK :, :BLK], block[2 * BLK :, BLK:]], axis=0)
    return jnp.concatenate([block[:BLK], high], axis=1)


def everywhere(block, after):
    along_z = [[(z * X + x) * C + c for z in range(Z)] for x in range(X) for c in range(C)]
    in_plane = [[(z * X + x) * C + c for x in range(X) for c in range(C)] for z in range(Z)]
    padded = jnp.pad(block, ((0, 0), (0, PADDED - PACK), (0, 0)))
    columns = lax.all_gather(padded, "seq", axis=0, tiled=True, axis_index_groups=along_z)
    columns, _ = lax.optimization_barrier((columns, after))
    return lax.all_gather(columns[:, :PACK], "seq", axis=0, tiled=True, axis_index_groups=in_plane)


def payload_kernel(wanted_ref, blocks_ref, out_ref):
    def one(t, carry):
        out_ref[t] = blocks_ref[wanted_ref[t, 0, 0]]
        return carry

    lax.fori_loop(0, out_ref.shape[0], one, 0, unroll=8)


def payload(wanted, blocks):
    tiles = wanted.shape[0]
    whole = lambda shape: pl.BlockSpec(shape, lambda i, w: (0, 0, 0))
    return pl.pallas_call(
        payload_kernel,
        grid_spec=pltpu.PrefetchScalarGridSpec(
            num_scalar_prefetch=1,
            grid=(1,),
            in_specs=[whole(blocks.shape)],
            out_specs=whole((tiles, PACK, DV)),
        ),
        out_shape=jax.ShapeDtypeStruct((tiles, PACK, DV), blocks.dtype),
        cost_estimate=pl.CostEstimate(flops=0, bytes_accessed=2 * tiles * PACK * DV * 2, transcendentals=0),
        compiler_params=pltpu.CompilerParams(vmem_limit_bytes=16 << 20),
        name="payload",
    )(wanted, blocks)


def coarse_kernel(
    info_ref, kv_ref, q_ref, gate_ref, out_ref, keys, values_t, scores
):
    n_chunks = X * C
    rows = Z * BLK

    @pl.when(pl.program_id(0) == 0)
    def _():
        def one(n, carry):
            at = pl.multiple_of(n * 2 * BLK, 2 * BLK)
            keys[pl.ds(at, BLK), :] = unpacked_keys(kv_ref.at[2 * n])
            keys[pl.ds(at + BLK, BLK), :] = unpacked_keys(kv_ref.at[2 * n + 1])
            v = jnp.concatenate([kv_ref[2 * n, BLK : 2 * BLK], kv_ref[2 * n + 1, BLK : 2 * BLK]], axis=0)
            values_t[:, pl.ds(at, 2 * BLK)] = v.T
            return carry

        lax.fori_loop(0, n_chunks * Z // 2, one, 0)

    q = jnp.concatenate([q_ref[0], q_ref[1]], axis=1)
    width = q.shape[1]
    late = 2 * BLK
    row = lax.broadcasted_iota(jnp.int32, (late, width), 0)
    lane = lax.broadcasted_iota(jnp.int32, (late, width), 1)
    token0 = (Z - 2 + row // BLK) * (X * C * BLK) + row % BLK
    query_pos = info_ref[0] + lane % TILE
    top = jnp.full((1, width), NEGATIVE, jnp.float32)
    for n in range(n_chunks):
        s = jnp.dot(keys[n * rows : (n + 1) * rows, :], q, preferred_element_type=jnp.float32)
        tail = jnp.where((token0 + n * BLK) * CSTRIDE + CLEN - 1 <= query_pos, s[rows - late :], NEGATIVE)
        scores[n * rows : (n + 1) * rows - late, :] = s[: rows - late]
        scores[(n + 1) * rows - late : (n + 1) * rows, :] = tail
        top = jnp.maximum(top, jnp.max(s[: rows - late], axis=0, keepdims=True))
        top = jnp.maximum(top, jnp.max(tail, axis=0, keepdims=True))
    total = jnp.zeros((1, width), jnp.float32)
    acc = jnp.zeros((DV, width), jnp.float32)
    for n in range(n_chunks):
        w = jnp.exp2((scores[n * rows : (n + 1) * rows, :] - top) * EXP_SCALE)
        total = total + jnp.sum(w, axis=0, keepdims=True)
        acc = acc + jnp.dot(
            values_t[:, n * rows : (n + 1) * rows], w.astype(jnp.bfloat16), preferred_element_type=jnp.float32
        )
    gate = jnp.concatenate([gate_ref[0], gate_ref[1]], axis=1)
    acc = acc * (gate / total)
    out_ref[0] = acc[:, :TILE]
    out_ref[1] = acc[:, TILE:]


def in_hbm(x):
    return pltpu.with_memory_space_constraint(x, pltpu.HBM)


def coarse_branch(info, coarse, queries_t, gate):
    heads = queries_t.shape[0]
    tokens = coarse.shape[0] * BLK
    pair = lambda shape: pl.BlockSpec((2, *shape), lambda p, i: (p, 0, 0))
    return pl.pallas_call(
        coarse_kernel,
        grid_spec=pltpu.PrefetchScalarGridSpec(
            num_scalar_prefetch=1,
            grid=(heads // 2,),
            in_specs=[
                pl.BlockSpec(coarse.shape, lambda p, i: (0, 0, 0), pipeline_mode=pl.Buffered(1)),
                pair((DQK, TILE)),
                pair((1, TILE)),
            ],
            out_specs=pair((DV, TILE)),
            scratch_shapes=[
                pltpu.VMEM((tokens, DQK), jnp.bfloat16),
                pltpu.VMEM((DV, tokens), jnp.bfloat16),
                pltpu.VMEM((tokens, 2 * TILE), jnp.float32),
            ],
        ),
        out_shape=jax.ShapeDtypeStruct((heads, DV, TILE), jnp.float32),
        cost_estimate=pl.CostEstimate(
            flops=2 * heads * TILE * tokens * (DQK + DV),
            bytes_accessed=tokens * (DQK + DV) * 2 + heads * TILE * (DQK * 2 + DV * 4),
            transcendentals=heads * TILE * tokens,
        ),
        compiler_params=pltpu.CompilerParams(vmem_limit_bytes=20 << 20),
        name="coarse",
    )(info, coarse, queries_t, gate)


def tail_kernel(n_grp, info_ref, incoming, q_ref, gate_ref, coarse_ref, weight_ref, *rest):
    outs, (queries, coarse, weight, keys, values_t, attended, in_sem, weight_sem) = rest[:n_grp], rest[n_grp:]
    heads = queries.shape[0]
    cols = weight.shape[2]
    base, grp = info_ref[0], info_ref[1]
    q_copy = pltpu.make_async_copy(q_ref, queries, in_sem.at[0])
    coarse_copy = pltpu.make_async_copy(coarse_ref, coarse, in_sem.at[1])
    q_copy.start()
    coarse_copy.start()
    late = SEL - 1
    for j in range(SEL):
        late = jnp.where(info_ref[3 + j] * BLK >= base, j, late)
    owners = []
    for j in range(SEL):
        slot_from = jnp.where(late == j, SEL - 1, j) if j < SEL - 1 else late
        owners.append(info_ref[3 + slot_from] // (1024 // BLK))
    for j in range(0, SEL, 2):
        first, second = incoming.at[owners[j]], incoming.at[owners[j + 1]]
        keys[j * BLK : (j + 1) * BLK, :] = unpacked_keys(first)
        keys[(j + 1) * BLK : (j + 2) * BLK, :] = unpacked_keys(second)
        v = jnp.concatenate([first[BLK : 2 * BLK], second[BLK : 2 * BLK]], axis=0)
        values_t[:, j * BLK : (j + 2) * BLK] = v.T
    q_copy.wait()
    coarse_copy.wait()
    weight_copies = []
    for k in range(n_grp):
        at = pl.multiple_of(lax.rem(grp + k, n_grp) * cols, DV)
        weight_copies.append(
            pltpu.make_async_copy(weight_ref.at[:, pl.ds(at, cols)], weight.at[k], weight_sem.at[k])
        )
    for copy in weight_copies:
        copy.start()
    width = 2 * TILE
    n_keys = SEL * BLK
    row = lax.broadcasted_iota(jnp.int32, (BLK, width), 0)
    lane = lax.broadcasted_iota(jnp.int32, (BLK, width), 1)
    seen = info_ref[3 + late] * BLK + row <= base + lane % TILE

    for p in range(heads // 2):
        q = jnp.concatenate([queries[2 * p], queries[2 * p + 1]], axis=1)
        s = jnp.dot(keys[...], q, preferred_element_type=jnp.float32)
        last = jnp.where(seen, s[n_keys - BLK :], NEGATIVE)
        top = jnp.maximum(
            jnp.max(s[: n_keys - BLK], axis=0, keepdims=True), jnp.max(last, axis=0, keepdims=True)
        )
        w = jnp.exp2((jnp.concatenate([s[: n_keys - BLK], last], axis=0) - top) * EXP_SCALE)
        total = jnp.sum(w, axis=0, keepdims=True)
        o = jnp.dot(values_t[...], w.astype(jnp.bfloat16), preferred_element_type=jnp.float32)
        gate = jnp.concatenate([gate_ref[2 * p], gate_ref[2 * p + 1]], axis=1)
        o = o * (gate / total)
        for i in range(2):
            h = 2 * p + i
            both = o[:, i * TILE : (i + 1) * TILE] + coarse[h]
            attended[:, h * DV : (h + 1) * DV] = both.T.astype(jnp.bfloat16)
    for k in (*range(1, n_grp), 0):
        weight_copies[k].wait()
        part = jnp.dot(attended[...], weight[k], preferred_element_type=jnp.float32)
        outs[k][...] = part.astype(outs[k].dtype)


def tail(info, incoming, queries_t, gate, coarse_out, out_weight, n_grp):
    heads = queries_t.shape[0]
    rows, model = out_weight.shape
    cols = model // n_grp
    vmem = lambda shape: pl.BlockSpec(shape, lambda i, s: (0,) * len(shape))
    on_chip = pl.BlockSpec(memory_space=pltpu.VMEM)
    hbm = pl.BlockSpec(memory_space=pltpu.HBM)
    return pl.pallas_call(
        functools.partial(tail_kernel, n_grp),
        grid_spec=pltpu.PrefetchScalarGridSpec(
            num_scalar_prefetch=1,
            grid=(1,),
            in_specs=[
                on_chip,
                hbm,
                vmem(gate.shape),
                hbm,
                hbm,
            ],
            out_specs=[vmem((TILE, cols))] * n_grp,
            scratch_shapes=[
                pltpu.VMEM(queries_t.shape, queries_t.dtype),
                pltpu.VMEM(coarse_out.shape, coarse_out.dtype),
                pltpu.VMEM((n_grp, rows, cols), jnp.bfloat16),
                pltpu.VMEM((SEL * BLK, DQK), jnp.bfloat16),
                pltpu.VMEM((DV, SEL * BLK), jnp.bfloat16),
                pltpu.VMEM((TILE, rows), jnp.bfloat16),
                pltpu.SemaphoreType.DMA((2,)),
                pltpu.SemaphoreType.DMA((n_grp,)),
            ],
        ),
        out_shape=[jax.ShapeDtypeStruct((TILE, cols), jnp.float32)]
        + [jax.ShapeDtypeStruct((TILE, cols), jnp.bfloat16)] * (n_grp - 1),
        cost_estimate=pl.CostEstimate(
            flops=2 * heads * TILE * SEL * BLK * (DQK + DV) + 2 * TILE * rows * model,
            bytes_accessed=rows * model * 2,
            transcendentals=heads * TILE * SEL * BLK,
        ),
        compiler_params=pltpu.CompilerParams(vmem_limit_bytes=24 << 20),
        name="tail",
    )(info, incoming, in_hbm(queries_t), gate, in_hbm(coarse_out), in_hbm(out_weight))


def shards(
    queries,
    key_cache,
    group_value_cache,
    coarse_keys,
    coarse_values,
    hidden,
    gate_weight,
    out_weight,
    selected,
):
    seq_count = lax.axis_size("seq")
    n_grp = lax.axis_size("grp")
    seq_index = lax.axis_index("seq")
    grp_index = lax.axis_index("grp")
    ctx_dev = key_cache.shape[1]
    context = ctx_dev * seq_count
    heads = queries.shape[1]
    blocks_dev = ctx_dev // BLK

    own_list = selected[0, 0]
    owners = jnp.arange(seq_count, dtype=jnp.int32)
    mine = (own_list[None, :] // blocks_dev == owners[:, None]).astype(jnp.int32)
    wanted = jnp.sum(mine * (own_list % blocks_dev)[None, :], axis=1)
    wanted = lax.all_to_all(wanted[:, None, None], "seq", 0, 0, tiled=True)

    blocks = packed_blocks(
        key_cache[0].reshape(blocks_dev, BLK, DQK), group_value_cache[0].reshape(blocks_dev, BLK, DV)
    )
    outgoing = payload(wanted, blocks)
    coarse = everywhere(packed_blocks(coarse_keys, coarse_values), outgoing)
    incoming = lax.all_to_all(outgoing, "seq", 0, 0, tiled=True)

    first_query = context - TILE * seq_count
    first_pos = first_query + seq_index * TILE
    info = jnp.concatenate([jnp.stack([first_pos, grp_index, seq_index]).astype(jnp.int32), own_list])
    queries_t = jnp.transpose(queries, (1, 2, 0))
    gates = jax.nn.sigmoid(
        lax.dot_general(
            gate_weight[0], hidden, (((0,), (1,)), ((), ())), preferred_element_type=jnp.float32
        )
    )[:, None, :]
    coarse_out = coarse_branch(info, coarse, queries_t, gates[:heads])
    own, *others = tail(info, incoming, queries_t, gates[heads:], coarse_out, out_weight, n_grp)
    for k, part in enumerate(others, 1):
        perm = [(i, (i + k) % n_grp) for i in range(n_grp)]
        own = own + lax.ppermute(part, "grp", perm).astype(jnp.float32)
    return own.astype(jnp.bfloat16)


def solution(mesh):
    return jax.shard_map(
        shards,
        mesh=mesh,
        in_specs=(
            P("seq", "grp", None),
            P("grp", "seq", None),
            P("grp", "seq", None),
            P("grp", "seq", None),
            P("grp", "seq", None),
            P("seq", None),
            P("grp", None, None),
            P("grp", None),
            P("grp", "seq", None),
        ),
        out_specs=P("seq", "grp"),
        check_vma=False,
    )
```

```python
import functools
import math

import jax
import jax.numpy as jnp
from jax import lax
from jax.experimental import pallas as pl
from jax.experimental.pallas import tpu as pltpu
from jax.sharding import PartitionSpec as P

BLK = 64
SEL = 16
TILE = 128
CSTRIDE = 16
CLEN = 32
DQK = 192
DV = 128
PACK = BLK + BLK + BLK // 2
LETTER = PACK + 8
OWNED = 16
EARLY = 16
NEGATIVE = -1e30
EXP_SCALE = DQK**-0.5 * math.log2(math.e)
Z, X, C = 8, 4, 2


def packed_blocks(keys, values):
    high = jnp.concatenate([keys[:, : BLK // 2, DV:], keys[:, BLK // 2 :, DV:]], axis=2)
    return jnp.concatenate([keys[:, :, :DV], values, high], axis=1)


def unpacked_keys(block):
    high = jnp.concatenate([block[2 * BLK : PACK, :BLK], block[2 * BLK : PACK, BLK:]], axis=0)
    return jnp.concatenate([block[:BLK], high], axis=1)


def index(z, x, c):
    return ((z % Z) * X + x % X) * C + c % C


SITES = [(z, x, c) for z in range(Z) for x in range(X) for c in range(C)]
ALONG_Z = [[index(z, x, c) for z in range(Z)] for x in range(X) for c in range(C)]
IN_PLANE = [[index(z, x, c) for x in range(X) for c in range(C)] for z in range(Z)]


def shifted(x, dx, dc):
    return lax.ppermute(x, "seq", [(index(*s), index(s[0], s[1] + dx, s[2] + dc)) for s in SITES])


def letter_kernel(list_ref, keys_ref, values_ref, out_ref):
    keys = keys_ref[0]
    high = jnp.concatenate([keys[: BLK // 2, DV:], keys[BLK // 2 :, DV:]], axis=1)
    lane = lax.broadcasted_iota(jnp.int32, (LETTER - PACK, DV), 1)
    for z in range(Z):
        out_ref[z, :BLK] = keys[:, :DV]
        out_ref[z, BLK : 2 * BLK] = values_ref[0]
        out_ref[z, 2 * BLK : PACK] = high
        wanted = jnp.zeros(lane.shape, jnp.float32)
        for j in range(SEL):
            block = list_ref[j]
            at = block // OWNED - z * (X * C)
            wanted = jnp.where(lane == at, (block % OWNED).astype(jnp.float32), wanted)
        out_ref[z, PACK:] = wanted.astype(jnp.bfloat16)


def letters(own_list, keys, values):
    return pl.pallas_call(
        letter_kernel,
        grid_spec=pltpu.PrefetchScalarGridSpec(
            num_scalar_prefetch=1,
            grid=(1,),
            in_specs=[pl.BlockSpec(a.shape, lambda i, s: (0, 0, 0)) for a in (keys, values)],
            out_specs=pl.BlockSpec((Z, LETTER, DV), lambda i, s: (0, 0, 0)),
        ),
        out_shape=jax.ShapeDtypeStruct((Z, LETTER, DV), keys.dtype),
        cost_estimate=pl.CostEstimate(flops=0, bytes_accessed=Z * LETTER * DV * 2, transcendentals=0),
        name="letters",
    )(own_list, keys, values)


def payload_kernel(wanted_ref, blocks_ref, out_ref):
    def one(t, carry):
        out_ref[t] = blocks_ref[wanted_ref[t % (X * C), 0, t // (X * C)]]
        return carry

    lax.fori_loop(0, out_ref.shape[0], one, 0, unroll=8)


def payload(wanted, blocks):
    tiles = wanted.shape[0] * wanted.shape[2]
    whole = lambda shape: pl.BlockSpec(shape, lambda i, w: (0, 0, 0))
    return pl.pallas_call(
        payload_kernel,
        grid_spec=pltpu.PrefetchScalarGridSpec(
            num_scalar_prefetch=1,
            grid=(1,),
            in_specs=[whole(blocks.shape)],
            out_specs=whole((tiles, PACK, DV)),
        ),
        out_shape=jax.ShapeDtypeStruct((tiles, PACK, DV), blocks.dtype),
        cost_estimate=pl.CostEstimate(flops=0, bytes_accessed=2 * tiles * PACK * DV * 2, transcendentals=0),
        compiler_params=pltpu.CompilerParams(vmem_limit_bytes=16 << 20),
        name="payload",
    )(wanted, blocks)


def coarse_kernel(info_ref, *rest):
    kv_refs, (q_ref, out_ref, lse_ref, keys, values_t, scores) = rest[:X], rest[X:]
    rows = Z * BLK
    base, x, c = info_ref[0], info_ref[1], info_ref[2]

    @pl.when(pl.program_id(0) == 0)
    def _():
        for n in range(X):
            kv_ref = kv_refs[n]
            for z in range(0, Z, 2):
                at = n * rows + z * BLK
                keys[at : at + BLK, :] = unpacked_keys(kv_ref.at[z])
                keys[at + BLK : at + 2 * BLK, :] = unpacked_keys(kv_ref.at[z + 1])
                v = jnp.concatenate([kv_ref[z, BLK : 2 * BLK], kv_ref[z + 1, BLK : 2 * BLK]], axis=0)
                values_t[:, at : at + 2 * BLK] = v.T

    q = jnp.concatenate([q_ref[0], q_ref[1]], axis=1)
    width = q.shape[1]
    late = 2 * BLK
    row = lax.broadcasted_iota(jnp.int32, (late, width), 0)
    lane = lax.broadcasted_iota(jnp.int32, (late, width), 1)
    token0 = (Z - 2 + row // BLK) * (X * C * BLK) + row % BLK
    query_pos = base + lane % TILE
    top = jnp.full((1, width), NEGATIVE, jnp.float32)
    for n in range(X):
        s = jnp.dot(keys[n * rows : (n + 1) * rows, :], q, preferred_element_type=jnp.float32)
        token = token0 + ((x + X - n) % X * C + c) * BLK
        tail = jnp.where(token * CSTRIDE + CLEN - 1 <= query_pos, s[rows - late :], NEGATIVE)
        scores[n * rows : (n + 1) * rows - late, :] = s[: rows - late]
        scores[(n + 1) * rows - late : (n + 1) * rows, :] = tail
        top = jnp.maximum(top, jnp.max(s[: rows - late], axis=0, keepdims=True))
        top = jnp.maximum(top, jnp.max(tail, axis=0, keepdims=True))
    total = jnp.zeros((1, width), jnp.float32)
    acc = jnp.zeros((DV, width), jnp.float32)
    for n in range(X):
        w = jnp.exp2((scores[n * rows : (n + 1) * rows, :] - top) * EXP_SCALE)
        total = total + jnp.sum(w, axis=0, keepdims=True)
        acc = acc + jnp.dot(
            values_t[:, n * rows : (n + 1) * rows], w.astype(jnp.bfloat16), preferred_element_type=jnp.float32
        )
    acc = acc * (1.0 / total)
    lse = top * EXP_SCALE + jnp.log(total) * math.log2(math.e)
    for i in range(2):
        out_ref[i] = acc[:, i * TILE : (i + 1) * TILE].astype(out_ref.dtype)
        lse_ref[i] = lse[:, i * TILE : (i + 1) * TILE]


def in_hbm(x):
    return pltpu.with_memory_space_constraint(x, pltpu.HBM)


def coarse_half(info, coarse, queries_t, dtype):
    heads = queries_t.shape[0]
    tokens = X * Z * BLK
    pair = lambda shape: pl.BlockSpec((2, *shape), lambda p, i: (p, 0, 0))
    return pl.pallas_call(
        coarse_kernel,
        grid_spec=pltpu.PrefetchScalarGridSpec(
            num_scalar_prefetch=1,
            grid=(heads // 2,),
            in_specs=[
                *[pl.BlockSpec(a.shape, lambda p, i: (0, 0, 0), pipeline_mode=pl.Buffered(1)) for a in coarse],
                pair((DQK, TILE)),
            ],
            out_specs=[pair((DV, TILE)), pair((1, TILE))],
            scratch_shapes=[
                pltpu.VMEM((tokens, DQK), jnp.bfloat16),
                pltpu.VMEM((DV, tokens), jnp.bfloat16),
                pltpu.VMEM((tokens, 2 * TILE), jnp.float32),
            ],
        ),
        out_shape=[
            jax.ShapeDtypeStruct((heads, DV, TILE), dtype),
            jax.ShapeDtypeStruct((heads, 1, TILE), jnp.float32),
        ],
        cost_estimate=pl.CostEstimate(
            flops=EARLY * 2 * heads * TILE * tokens * (DQK + DV),
            bytes_accessed=tokens * (DQK + DV) * 2 + heads * TILE * (DQK * 2 + DV * 4),
            transcendentals=EARLY * heads * TILE * tokens,
        ),
        compiler_params=pltpu.CompilerParams(vmem_limit_bytes=20 << 20),
        name="coarse",
    )(info, *coarse, queries_t)


def tail_kernel(n_grp, info_ref, incoming, q_ref, gate_ref, lse_ref, lse2_ref, coarse_ref, coarse2_ref, weight_ref, *rest):
    outs, scratch = rest[:n_grp], rest[n_grp:]
    queries, coarse, coarse2, weight, keys, values_t, attended, in_sem, weight_sem = scratch
    heads = queries.shape[0]
    cols = weight.shape[2]
    base, grp = info_ref[0], info_ref[1]
    q_copy = pltpu.make_async_copy(q_ref, queries, in_sem.at[0])
    coarse_copy = pltpu.make_async_copy(coarse_ref, coarse, in_sem.at[1])
    coarse2_copy = pltpu.make_async_copy(coarse2_ref, coarse2, in_sem.at[2])
    q_copy.start()
    coarse_copy.start()
    coarse2_copy.start()
    late = SEL - 1
    for j in range(SEL):
        late = jnp.where(info_ref[3 + j] * BLK >= base, j, late)
    owners = []
    for j in range(SEL):
        slot_from = jnp.where(late == j, SEL - 1, j) if j < SEL - 1 else late
        owners.append(info_ref[3 + slot_from] // OWNED)
    for j in range(0, SEL, 2):
        first, second = incoming.at[owners[j]], incoming.at[owners[j + 1]]
        keys[j * BLK : (j + 1) * BLK, :] = unpacked_keys(first)
        keys[(j + 1) * BLK : (j + 2) * BLK, :] = unpacked_keys(second)
        v = jnp.concatenate([first[BLK : 2 * BLK], second[BLK : 2 * BLK]], axis=0)
        values_t[:, j * BLK : (j + 2) * BLK] = v.T
    q_copy.wait()
    coarse_copy.wait()
    coarse2_copy.wait()
    weight_copies = []
    for k in range(n_grp):
        at = pl.multiple_of(lax.rem(grp + k, n_grp) * cols, DV)
        weight_copies.append(
            pltpu.make_async_copy(weight_ref.at[:, pl.ds(at, cols)], weight.at[k], weight_sem.at[k])
        )
    for copy in weight_copies:
        copy.start()
    width = 2 * TILE
    n_keys = SEL * BLK
    row = lax.broadcasted_iota(jnp.int32, (BLK, width), 0)
    lane = lax.broadcasted_iota(jnp.int32, (BLK, width), 1)
    seen = info_ref[3 + late] * BLK + row <= base + lane % TILE

    for p in range(heads // 2):
        q = jnp.concatenate([queries[2 * p], queries[2 * p + 1]], axis=1)
        s = jnp.dot(keys[...], q, preferred_element_type=jnp.float32)
        last = jnp.where(seen, s[n_keys - BLK :], NEGATIVE)
        top = jnp.maximum(
            jnp.max(s[: n_keys - BLK], axis=0, keepdims=True), jnp.max(last, axis=0, keepdims=True)
        )
        w = jnp.exp2((jnp.concatenate([s[: n_keys - BLK], last], axis=0) - top) * EXP_SCALE)
        total = jnp.sum(w, axis=0, keepdims=True)
        o = jnp.dot(values_t[...], w.astype(jnp.bfloat16), preferred_element_type=jnp.float32)
        gate = jnp.concatenate([gate_ref[heads + 2 * p], gate_ref[heads + 2 * p + 1]], axis=1)
        o = o * (gate / total)
        for i in range(2):
            h = 2 * p + i
            gap = lse2_ref[h] - lse_ref[h]
            both = o[:, i * TILE : (i + 1) * TILE] + coarse[h] * (gate_ref[h] / (1.0 + jnp.exp2(gap)))
            both = both + coarse2[h].astype(jnp.float32) * (gate_ref[h] / (1.0 + jnp.exp2(-gap)))
            attended[:, h * DV : (h + 1) * DV] = both.T.astype(jnp.bfloat16)
    for k in (*range(1, n_grp), 0):
        weight_copies[k].wait()
        part = jnp.dot(attended[...], weight[k], preferred_element_type=jnp.float32)
        outs[k][...] = part.astype(outs[k].dtype)


def tail(info, incoming, queries_t, gate, coarse, coarse2, out_weight, n_grp):
    heads = queries_t.shape[0]
    rows, model = out_weight.shape
    cols = model // n_grp
    vmem = lambda shape: pl.BlockSpec(shape, lambda i, s: (0,) * len(shape))
    on_chip = pl.BlockSpec(memory_space=pltpu.VMEM)
    hbm = pl.BlockSpec(memory_space=pltpu.HBM)
    return pl.pallas_call(
        functools.partial(tail_kernel, n_grp),
        grid_spec=pltpu.PrefetchScalarGridSpec(
            num_scalar_prefetch=1,
            grid=(1,),
            in_specs=[
                on_chip,
                hbm,
                vmem(gate.shape),
                vmem(coarse[1].shape),
                vmem(coarse[1].shape),
                hbm,
                hbm,
                hbm,
            ],
            out_specs=[vmem((TILE, cols))] * n_grp,
            scratch_shapes=[
                pltpu.VMEM(queries_t.shape, queries_t.dtype),
                pltpu.VMEM(coarse[0].shape, coarse[0].dtype),
                pltpu.VMEM(coarse2[0].shape, coarse2[0].dtype),
                pltpu.VMEM((n_grp, rows, cols), jnp.bfloat16),
                pltpu.VMEM((SEL * BLK, DQK), jnp.bfloat16),
                pltpu.VMEM((DV, SEL * BLK), jnp.bfloat16),
                pltpu.VMEM((TILE, rows), jnp.bfloat16),
                pltpu.SemaphoreType.DMA((3,)),
                pltpu.SemaphoreType.DMA((n_grp,)),
            ],
        ),
        out_shape=[jax.ShapeDtypeStruct((TILE, cols), jnp.float32)]
        + [jax.ShapeDtypeStruct((TILE, cols), jnp.bfloat16)] * (n_grp - 1),
        cost_estimate=pl.CostEstimate(
            flops=2 * heads * TILE * SEL * BLK * (DQK + DV) + 2 * TILE * rows * model,
            bytes_accessed=rows * model * 2,
            transcendentals=heads * TILE * SEL * BLK,
        ),
        compiler_params=pltpu.CompilerParams(vmem_limit_bytes=24 << 20),
        name="tail",
    )(
        info,
        incoming,
        in_hbm(queries_t),
        gate,
        coarse[1],
        coarse2[1],
        in_hbm(coarse[0]),
        in_hbm(coarse2[0]),
        in_hbm(out_weight),
    )


def shards(
    queries,
    key_cache,
    group_value_cache,
    coarse_keys,
    coarse_values,
    hidden,
    gate_weight,
    out_weight,
    selected,
):
    seq_count = lax.axis_size("seq")
    n_grp = lax.axis_size("grp")
    seq_index = lax.axis_index("seq")
    grp_index = lax.axis_index("grp")
    ctx_dev = key_cache.shape[1]
    context = ctx_dev * seq_count
    heads = queries.shape[1]
    blocks_dev = ctx_dev // BLK

    own_list = selected[0, 0]
    queries_t = jnp.transpose(queries, (1, 2, 0))
    other_q = shifted(queries_t, 0, 1)

    came = lax.all_to_all(
        letters(own_list, coarse_keys, coarse_values), "seq", 0, 0, axis_index_groups=ALONG_Z, tiled=True
    )
    wanted = jnp.transpose(came[:, PACK, : X * C])[:, None, :].astype(jnp.int32)
    wanted = lax.all_to_all(wanted, "seq", 0, 0, axis_index_groups=IN_PLANE, tiled=True)

    column, wanted, other_q = lax.optimization_barrier((came, wanted, other_q))
    coarse = [column] + [shifted(column, k, 0) for k in range(1, X)]

    blocks = packed_blocks(
        key_cache[0].reshape(blocks_dev, BLK, DQK), group_value_cache[0].reshape(blocks_dev, BLK, DV)
    )
    incoming = lax.all_to_all(payload(wanted, blocks), "seq", 0, 0, tiled=True)

    first_query = context - TILE * seq_count
    x_index, c_index = seq_index // C % X, seq_index % C
    scalars = lambda *values: jnp.stack(values).astype(jnp.int32)
    other_index = seq_index + 1 - 2 * c_index
    gates = jax.nn.sigmoid(
        lax.dot_general(
            gate_weight[0], hidden, (((0,), (1,)), ((), ())), preferred_element_type=jnp.float32
        )
    )[:, None, :]
    first_pos = first_query + seq_index * TILE
    theirs = coarse_half(scalars(first_query + other_index * TILE, x_index, c_index), coarse, other_q, jnp.bfloat16)
    coarse2 = [shifted(a, 0, 1) for a in theirs]
    coarse1 = coarse_half(scalars(first_pos, x_index, c_index), coarse, queries_t, jnp.float32)
    info = jnp.concatenate([scalars(first_pos, grp_index, seq_index), own_list])
    own, *others = tail(info, incoming, queries_t, gates, coarse1, coarse2, out_weight, n_grp)
    for k, part in enumerate(others, 1):
        perm = [(i, (i + k) % n_grp) for i in range(n_grp)]
        own = own + lax.ppermute(part, "grp", perm).astype(jnp.float32)
    return own.astype(jnp.bfloat16)


def solution(mesh):
    return jax.shard_map(
        shards,
        mesh=mesh,
        in_specs=(
            P("seq", "grp", None),
            P("grp", "seq", None),
            P("grp", "seq", None),
            P("grp", "seq", None),
            P("grp", "seq", None),
            P("seq", None),
            P("grp", None, None),
            P("grp", None),
            P("grp", "seq", None),
        ),
        out_specs=P("seq", "grp"),
        check_vma=False,
    )
```

```python
import functools
import math

import jax
import jax.numpy as jnp
from jax import lax
from jax.experimental import pallas as pl
from jax.experimental.pallas import tpu as pltpu
from jax.sharding import PartitionSpec as P

BLK = 64
SEL = 16
TILE = 128
CSTRIDE = 16
CLEN = 32
DQK = 192
DV = 128
PACK = BLK + BLK + BLK // 2
LETTER = PACK + 8
OWNED_BITS = 4
OWNED = 1 << OWNED_BITS
EARLY = 16
NEGATIVE = -1e30
EXP_SCALE = DQK**-0.5 * math.log2(math.e)
Z, X, C = 8, 4, 2


def packed_blocks(keys, values):
    high = jnp.concatenate([keys[:, : BLK // 2, DV:], keys[:, BLK // 2 :, DV:]], axis=2)
    return jnp.concatenate([keys[:, :, :DV], values, high], axis=1)


def unpacked_keys(block):
    high = jnp.concatenate([block[2 * BLK : PACK, :BLK], block[2 * BLK : PACK, BLK:]], axis=0)
    return jnp.concatenate([block[:BLK], high], axis=1)


def index(z, x, c):
    return ((z % Z) * X + x % X) * C + c % C


SITES = [(z, x, c) for z in range(Z) for x in range(X) for c in range(C)]
ALONG_Z = [[index(z, x, c) for z in range(Z)] for x in range(X) for c in range(C)]
IN_PLANE = [[index(z, x, c) for x in range(X) for c in range(C)] for z in range(Z)]


def shifted(x, dx, dc):
    return lax.ppermute(x, "seq", [(index(*s), index(s[0], s[1] + dx, s[2] + dc)) for s in SITES])


def letter_kernel(list_ref, keys_ref, values_ref, out_ref):
    keys = keys_ref[0]
    high = jnp.concatenate([keys[: BLK // 2, DV:], keys[BLK // 2 :, DV:]], axis=1)
    lane = lax.broadcasted_iota(jnp.int32, (LETTER - PACK, DV), 1)
    wishes = [(list_ref[j] >> OWNED_BITS, (list_ref[j] & (OWNED - 1)).astype(jnp.float32)) for j in range(SEL)]
    for z in range(Z):
        out_ref[z, :BLK] = keys[:, :DV]
        out_ref[z, BLK : 2 * BLK] = values_ref[0]
        out_ref[z, 2 * BLK : PACK] = high
        wanted = jnp.zeros(lane.shape, jnp.float32)
        for owner, block in wishes:
            wanted = jnp.where(lane == owner - z * (X * C), block, wanted)
        out_ref[z, PACK:] = wanted.astype(jnp.bfloat16)


def letters(own_list, keys, values):
    return pl.pallas_call(
        letter_kernel,
        grid_spec=pltpu.PrefetchScalarGridSpec(
            num_scalar_prefetch=1,
            grid=(1,),
            in_specs=[pl.BlockSpec(a.shape, lambda i, s: (0, 0, 0)) for a in (keys, values)],
            out_specs=pl.BlockSpec((Z, LETTER, DV), lambda i, s: (0, 0, 0)),
        ),
        out_shape=jax.ShapeDtypeStruct((Z, LETTER, DV), keys.dtype),
        cost_estimate=pl.CostEstimate(flops=0, bytes_accessed=Z * LETTER * DV * 2, transcendentals=0),
        name="letters",
    )(own_list, keys, values)


def payload_kernel(wanted_ref, blocks_ref, out_ref):
    z0 = pl.program_id(0) * (out_ref.shape[0] // (X * C))
    for t in range(out_ref.shape[0]):
        z, at = divmod(t, X * C)
        out_ref[t] = blocks_ref[wanted_ref[at, 0, z0 + z]]


def payload(wanted, blocks):
    tiles = wanted.shape[0] * wanted.shape[2]
    steps = 4
    return pl.pallas_call(
        payload_kernel,
        grid_spec=pltpu.PrefetchScalarGridSpec(
            num_scalar_prefetch=1,
            grid=(steps,),
            in_specs=[pl.BlockSpec(blocks.shape, lambda i, w: (0, 0, 0))],
            out_specs=pl.BlockSpec((tiles // steps, PACK, DV), lambda i, w: (i, 0, 0)),
        ),
        out_shape=jax.ShapeDtypeStruct((tiles, PACK, DV), blocks.dtype),
        cost_estimate=pl.CostEstimate(flops=0, bytes_accessed=2 * tiles * PACK * DV * 2, transcendentals=0),
        compiler_params=pltpu.CompilerParams(vmem_limit_bytes=16 << 20),
        name="payload",
    )(wanted, blocks)


def coarse_kernel(info_ref, *rest):
    kv_refs, (q_ref, out_ref, lse_ref, keys, values_t, scores) = rest[:X], rest[X:]
    rows = Z * BLK
    base, x, c = info_ref[0], info_ref[1], info_ref[2]

    @pl.when(pl.program_id(0) == 0)
    def _():
        for n in range(X):
            kv_ref = kv_refs[n]
            for z in range(0, Z, 2):
                at = n * rows + z * BLK
                keys[at : at + BLK, :] = unpacked_keys(kv_ref.at[z])
                keys[at + BLK : at + 2 * BLK, :] = unpacked_keys(kv_ref.at[z + 1])
                v = jnp.concatenate([kv_ref[z, BLK : 2 * BLK], kv_ref[z + 1, BLK : 2 * BLK]], axis=0)
                values_t[:, at : at + 2 * BLK] = v.T

    q = jnp.concatenate([q_ref[0], q_ref[1]], axis=1)
    width = q.shape[1]
    late = 2 * BLK
    row = lax.broadcasted_iota(jnp.int32, (late, width), 0)
    lane = lax.broadcasted_iota(jnp.int32, (late, width), 1)
    token0 = (Z - 2 + row // BLK) * (X * C * BLK) + row % BLK
    query_pos = base + lane % TILE
    top = jnp.full((1, width), NEGATIVE, jnp.float32)
    for n in range(X):
        s = jnp.dot(keys[n * rows : (n + 1) * rows, :], q, preferred_element_type=jnp.float32)
        token = token0 + ((x + X - n) % X * C + c) * BLK
        tail = jnp.where(token * CSTRIDE + CLEN - 1 <= query_pos, s[rows - late :], NEGATIVE)
        scores[n * rows : (n + 1) * rows - late, :] = s[: rows - late]
        scores[(n + 1) * rows - late : (n + 1) * rows, :] = tail
        top = jnp.maximum(top, jnp.max(s[: rows - late], axis=0, keepdims=True))
        top = jnp.maximum(top, jnp.max(tail, axis=0, keepdims=True))
    total = jnp.zeros((1, width), jnp.float32)
    acc = jnp.zeros((DV, width), jnp.float32)
    for n in range(X):
        w = jnp.exp2((scores[n * rows : (n + 1) * rows, :] - top) * EXP_SCALE)
        total = total + jnp.sum(w, axis=0, keepdims=True)
        acc = acc + jnp.dot(
            values_t[:, n * rows : (n + 1) * rows], w.astype(jnp.bfloat16), preferred_element_type=jnp.float32
        )
    acc = acc * (1.0 / total)
    lse = top * EXP_SCALE + jnp.log(total) * math.log2(math.e)
    for i in range(2):
        out_ref[i] = acc[:, i * TILE : (i + 1) * TILE].astype(out_ref.dtype)
        lse_ref[i] = lse[:, i * TILE : (i + 1) * TILE]


def in_hbm(x):
    return pltpu.with_memory_space_constraint(x, pltpu.HBM)


def coarse_half(info, coarse, queries_t, dtype):
    heads = queries_t.shape[0]
    tokens = X * Z * BLK
    pair = lambda shape: pl.BlockSpec((2, *shape), lambda p, i: (p, 0, 0))
    return pl.pallas_call(
        coarse_kernel,
        grid_spec=pltpu.PrefetchScalarGridSpec(
            num_scalar_prefetch=1,
            grid=(heads // 2,),
            in_specs=[
                *[pl.BlockSpec(a.shape, lambda p, i: (0, 0, 0), pipeline_mode=pl.Buffered(1)) for a in coarse],
                pair((DQK, TILE)),
            ],
            out_specs=[pair((DV, TILE)), pair((1, TILE))],
            scratch_shapes=[
                pltpu.VMEM((tokens, DQK), jnp.bfloat16),
                pltpu.VMEM((DV, tokens), jnp.bfloat16),
                pltpu.VMEM((tokens, 2 * TILE), jnp.float32),
            ],
        ),
        out_shape=[
            jax.ShapeDtypeStruct((heads, DV, TILE), dtype),
            jax.ShapeDtypeStruct((heads, 1, TILE), jnp.float32),
        ],
        cost_estimate=pl.CostEstimate(
            flops=EARLY * 2 * heads * TILE * tokens * (DQK + DV),
            bytes_accessed=tokens * (DQK + DV) * 2 + heads * TILE * (DQK * 2 + DV * 4),
            transcendentals=EARLY * heads * TILE * tokens,
        ),
        compiler_params=pltpu.CompilerParams(vmem_limit_bytes=20 << 20),
        name="coarse",
    )(info, *coarse, queries_t)


def tail_kernel(n_grp, info_ref, incoming, q_ref, gate_ref, lse_ref, lse2_ref, coarse_ref, coarse2_ref, weight_ref, *rest):
    outs, scratch = rest[:n_grp], rest[n_grp:]
    queries, coarse, coarse2, weight, keys, values_t, attended, in_sem, weight_sem = scratch
    heads = queries.shape[0]
    cols = weight.shape[1] // n_grp
    base, grp = info_ref[0], info_ref[1]
    q_copy = pltpu.make_async_copy(q_ref, queries, in_sem.at[0])
    coarse_copy = pltpu.make_async_copy(coarse_ref, coarse, in_sem.at[1])
    coarse2_copy = pltpu.make_async_copy(coarse2_ref, coarse2, in_sem.at[2])
    q_copy.start()
    coarse_copy.start()
    coarse2_copy.start()
    late = SEL - 1
    for j in range(SEL):
        late = jnp.where(info_ref[3 + j] * BLK >= base, j, late)
    owners = []
    for j in range(SEL):
        slot_from = jnp.where(late == j, SEL - 1, j) if j < SEL - 1 else late
        owners.append(info_ref[3 + slot_from] >> OWNED_BITS)
    for j in range(0, SEL, 2):
        first, second = incoming.at[owners[j]], incoming.at[owners[j + 1]]
        keys[j * BLK : (j + 1) * BLK, :] = unpacked_keys(first)
        keys[(j + 1) * BLK : (j + 2) * BLK, :] = unpacked_keys(second)
        v = jnp.concatenate([first[BLK : 2 * BLK], second[BLK : 2 * BLK]], axis=0)
        values_t[:, j * BLK : (j + 2) * BLK] = v.T
    q_copy.wait()
    coarse_copy.wait()
    coarse2_copy.wait()
    n_copies = weight_sem.shape[0]
    per_copy = weight.shape[0] // n_copies
    weight_copies = []
    for k in range(n_copies):
        rows = pl.ds(k * per_copy, per_copy)
        weight_copies.append(pltpu.make_async_copy(weight_ref.at[rows], weight.at[rows], weight_sem.at[k]))
    for copy in weight_copies:
        copy.start()
    width = 2 * TILE
    n_keys = SEL * BLK
    row = lax.broadcasted_iota(jnp.int32, (BLK, width), 0)
    lane = lax.broadcasted_iota(jnp.int32, (BLK, width), 1)
    seen = info_ref[3 + late] * BLK + row <= base + lane % TILE

    piece = 2 * BLK
    for p in range(heads // 2):
        q = jnp.concatenate([queries[2 * p], queries[2 * p + 1]], axis=1)
        top = jnp.full((1, width), NEGATIVE, jnp.float32)
        pieces = []
        for at in range(0, n_keys, piece):
            s = jnp.dot(keys[at : at + piece, :], q, preferred_element_type=jnp.float32)
            if at + piece == n_keys:
                s = jnp.concatenate([s[: piece - BLK], jnp.where(seen, s[piece - BLK :], NEGATIVE)], axis=0)
            pieces.append(s)
            top = jnp.maximum(top, jnp.max(s, axis=0, keepdims=True))
        top = top * EXP_SCALE
        total = jnp.zeros((1, width), jnp.float32)
        o = jnp.zeros((DV, width), jnp.float32)
        for n, s in enumerate(pieces):
            w = jnp.exp2(s * EXP_SCALE - top)
            total = total + jnp.sum(w, axis=0, keepdims=True)
            o = o + jnp.dot(
                values_t[:, n * piece : (n + 1) * piece], w.astype(jnp.bfloat16), preferred_element_type=jnp.float32
            )
        gate = jnp.concatenate([gate_ref[heads + 2 * p], gate_ref[heads + 2 * p + 1]], axis=1)
        o = o * (gate / total)
        both = []
        for i in range(2):
            h = 2 * p + i
            gap = lse2_ref[h] - lse_ref[h]
            out = o[:, i * TILE : (i + 1) * TILE] + coarse[h] * (gate_ref[h] / (1.0 + jnp.exp2(gap)))
            out = out + coarse2[h].astype(jnp.float32) * (gate_ref[h] / (1.0 + jnp.exp2(-gap)))
            both.append(out.T.astype(jnp.bfloat16))
        attended[:, 2 * p * DV : 2 * (p + 1) * DV] = jnp.concatenate(both, axis=1)
    for copy in weight_copies:
        copy.wait()
    for k in (*range(1, n_grp), 0):
        at = pl.multiple_of(lax.rem(grp + k, n_grp) * cols, DV)
        part = jnp.dot(attended[...], weight[:, pl.ds(at, cols)], preferred_element_type=jnp.float32)
        outs[k][...] = part.astype(outs[k].dtype)


def tail(info, incoming, queries_t, gate, coarse, coarse2, out_weight, n_grp):
    heads = queries_t.shape[0]
    rows, model = out_weight.shape
    cols = model // n_grp
    vmem = lambda shape: pl.BlockSpec(shape, lambda i, s: (0,) * len(shape))
    on_chip = pl.BlockSpec(memory_space=pltpu.VMEM)
    hbm = pl.BlockSpec(memory_space=pltpu.HBM)
    return pl.pallas_call(
        functools.partial(tail_kernel, n_grp),
        grid_spec=pltpu.PrefetchScalarGridSpec(
            num_scalar_prefetch=1,
            grid=(1,),
            in_specs=[
                on_chip,
                hbm,
                vmem(gate.shape),
                vmem(coarse[1].shape),
                vmem(coarse[1].shape),
                hbm,
                hbm,
                hbm,
            ],
            out_specs=[vmem((TILE, cols))] * n_grp,
            scratch_shapes=[
                pltpu.VMEM(queries_t.shape, queries_t.dtype),
                pltpu.VMEM(coarse[0].shape, coarse[0].dtype),
                pltpu.VMEM(coarse2[0].shape, coarse2[0].dtype),
                pltpu.VMEM((rows, model), jnp.bfloat16),
                pltpu.VMEM((SEL * BLK, DQK), jnp.bfloat16),
                pltpu.VMEM((DV, SEL * BLK), jnp.bfloat16),
                pltpu.VMEM((TILE, rows), jnp.bfloat16),
                pltpu.SemaphoreType.DMA((3,)),
                pltpu.SemaphoreType.DMA((4,)),
            ],
        ),
        out_shape=[jax.ShapeDtypeStruct((TILE, cols), jnp.float32)]
        + [jax.ShapeDtypeStruct((TILE, cols), jnp.bfloat16)] * (n_grp - 1),
        cost_estimate=pl.CostEstimate(
            flops=2 * heads * TILE * SEL * BLK * (DQK + DV) + 2 * TILE * rows * model,
            bytes_accessed=rows * model * 2,
            transcendentals=heads * TILE * SEL * BLK,
        ),
        compiler_params=pltpu.CompilerParams(vmem_limit_bytes=24 << 20),
        name="tail",
    )(
        info,
        incoming,
        in_hbm(queries_t),
        gate,
        coarse[1],
        coarse2[1],
        in_hbm(coarse[0]),
        in_hbm(coarse2[0]),
        in_hbm(out_weight),
    )


def shards(
    queries,
    key_cache,
    group_value_cache,
    coarse_keys,
    coarse_values,
    hidden,
    gate_weight,
    out_weight,
    selected,
):
    seq_count = lax.axis_size("seq")
    n_grp = lax.axis_size("grp")
    seq_index = lax.axis_index("seq")
    grp_index = lax.axis_index("grp")
    ctx_dev = key_cache.shape[1]
    context = ctx_dev * seq_count
    heads = queries.shape[1]
    blocks_dev = ctx_dev // BLK

    own_list = selected[0, 0]
    queries_t = jnp.transpose(queries, (1, 2, 0))
    other_q = shifted(queries_t, 0, 1)

    came = lax.all_to_all(
        letters(own_list, coarse_keys, coarse_values), "seq", 0, 0, axis_index_groups=ALONG_Z, tiled=True
    )
    wanted = jnp.transpose(came[:, PACK, : X * C])[:, None, :].astype(jnp.int32)
    wanted = lax.all_to_all(wanted, "seq", 0, 0, axis_index_groups=IN_PLANE, tiled=True)

    column, wanted, other_q = lax.optimization_barrier((came, wanted, other_q))
    coarse = [column] + [shifted(column, k, 0) for k in range(1, X)]

    blocks = packed_blocks(
        key_cache[0].reshape(blocks_dev, BLK, DQK), group_value_cache[0].reshape(blocks_dev, BLK, DV)
    )
    incoming = lax.all_to_all(payload(wanted, blocks), "seq", 0, 0, tiled=True)

    first_query = context - TILE * seq_count
    x_index, c_index = seq_index // C % X, seq_index % C
    scalars = lambda *values: jnp.stack(values).astype(jnp.int32)
    other_index = seq_index + 1 - 2 * c_index
    gates = jax.nn.sigmoid(
        lax.dot_general(
            gate_weight[0], hidden, (((0,), (1,)), ((), ())), preferred_element_type=jnp.float32
        )
    )[:, None, :]
    first_pos = first_query + seq_index * TILE
    theirs = coarse_half(scalars(first_query + other_index * TILE, x_index, c_index), coarse, other_q, jnp.bfloat16)
    coarse2 = [shifted(a, 0, 1) for a in theirs]
    coarse1 = coarse_half(scalars(first_pos, x_index, c_index), coarse, queries_t, jnp.float32)
    info = jnp.concatenate([scalars(first_pos, grp_index, seq_index), own_list])
    own, *others = tail(info, incoming, queries_t, gates, coarse1, coarse2, out_weight, n_grp)
    for k, part in enumerate(others, 1):
        perm = [(i, (i + k) % n_grp) for i in range(n_grp)]
        own = own + lax.ppermute(part, "grp", perm).astype(jnp.float32)
    return own.astype(jnp.bfloat16)


def solution(mesh):
    return jax.shard_map(
        shards,
        mesh=mesh,
        in_specs=(
            P("seq", "grp", None),
            P("grp", "seq", None),
            P("grp", "seq", None),
            P("grp", "seq", None),
            P("grp", "seq", None),
            P("seq", None),
            P("grp", None, None),
            P("grp", None),
            P("grp", "seq", None),
        ),
        out_specs=P("seq", "grp"),
        check_vma=False,
    )
```

```python
import functools
import math

import jax
import jax.numpy as jnp
from jax import lax
from jax.experimental import pallas as pl
from jax.experimental.pallas import tpu as pltpu
from jax.sharding import PartitionSpec as P

BLK = 64
SEL = 16
TILE = 128
CSTRIDE = 16
CLEN = 32
DQK = 192
DV = 128
PACK = BLK + BLK + BLK // 2
LETTER = PACK + 8
OWNED_BITS = 4
OWNED = 1 << OWNED_BITS
EARLY = 9.62
NEGATIVE = -1e30
EXP_SCALE = DQK**-0.5 * math.log2(math.e)
Z, X, C = 8, 4, 2


def packed_blocks(keys, values):
    high = jnp.concatenate([keys[:, : BLK // 2, DV:], keys[:, BLK // 2 :, DV:]], axis=2)
    return jnp.concatenate([keys[:, :, :DV], values, high], axis=1)


def unpacked_keys(block):
    high = jnp.concatenate([block[2 * BLK : PACK, :BLK], block[2 * BLK : PACK, BLK:]], axis=0)
    return jnp.concatenate([block[:BLK], high], axis=1)


def index(z, x, c):
    return ((z % Z) * X + x % X) * C + c % C


SITES = [(z, x, c) for z in range(Z) for x in range(X) for c in range(C)]
ALONG_Z = [[index(z, x, c) for z in range(Z)] for x in range(X) for c in range(C)]
IN_PLANE = [[index(z, x, c) for x in range(X) for c in range(C)] for z in range(Z)]


def shifted(x, dx, dc):
    return lax.ppermute(x, "seq", [(index(*s), index(s[0], s[1] + dx, s[2] + dc)) for s in SITES])


def letter_kernel(list_ref, keys_ref, values_ref, out_ref):
    keys = keys_ref[0]
    high = jnp.concatenate([keys[: BLK // 2, DV:], keys[BLK // 2 :, DV:]], axis=1)
    lane = lax.broadcasted_iota(jnp.int32, (LETTER - PACK, DV), 1)
    wishes = [(list_ref[j] >> OWNED_BITS, (list_ref[j] & (OWNED - 1)).astype(jnp.float32)) for j in range(SEL)]
    for z in range(Z):
        out_ref[z, :BLK] = keys[:, :DV]
        out_ref[z, BLK : 2 * BLK] = values_ref[0]
        out_ref[z, 2 * BLK : PACK] = high
        wanted = jnp.zeros(lane.shape, jnp.float32)
        for owner, block in wishes:
            wanted = jnp.where(lane == owner - z * (X * C), block, wanted)
        out_ref[z, PACK:] = wanted.astype(jnp.bfloat16)


def letters(own_list, keys, values):
    return pl.pallas_call(
        letter_kernel,
        grid_spec=pltpu.PrefetchScalarGridSpec(
            num_scalar_prefetch=1,
            grid=(1,),
            in_specs=[pl.BlockSpec(a.shape, lambda i, s: (0, 0, 0)) for a in (keys, values)],
            out_specs=pl.BlockSpec((Z, LETTER, DV), lambda i, s: (0, 0, 0)),
        ),
        out_shape=jax.ShapeDtypeStruct((Z, LETTER, DV), keys.dtype),
        cost_estimate=pl.CostEstimate(flops=0, bytes_accessed=Z * LETTER * DV * 2, transcendentals=0),
        name="letters",
    )(own_list, keys, values)


def payload_kernel(wanted_ref, blocks_ref, out_ref):
    z0 = pl.program_id(0) * (out_ref.shape[0] // (X * C))
    for t in range(out_ref.shape[0]):
        z, at = divmod(t, X * C)
        out_ref[t] = blocks_ref[wanted_ref[at, 0, z0 + z]]


def payload(wanted, blocks):
    tiles = wanted.shape[0] * wanted.shape[2]
    steps = 4
    return pl.pallas_call(
        payload_kernel,
        grid_spec=pltpu.PrefetchScalarGridSpec(
            num_scalar_prefetch=1,
            grid=(steps,),
            in_specs=[pl.BlockSpec(blocks.shape, lambda i, w: (0, 0, 0))],
            out_specs=pl.BlockSpec((tiles // steps, PACK, DV), lambda i, w: (i, 0, 0)),
        ),
        out_shape=jax.ShapeDtypeStruct((tiles, PACK, DV), blocks.dtype),
        cost_estimate=pl.CostEstimate(flops=0, bytes_accessed=2 * tiles * PACK * DV * 2, transcendentals=0),
        compiler_params=pltpu.CompilerParams(vmem_limit_bytes=16 << 20),
        name="payload",
    )(wanted, blocks)


def coarse_kernel(info_ref, *rest):
    kv_refs, (q_ref, out_ref, lse_ref, keys, values_t, scores) = rest[:X], rest[X:]
    rows = Z * BLK
    base, x, c = info_ref[0], info_ref[1], info_ref[2]

    @pl.when(pl.program_id(0) == 0)
    def _():
        for n in range(X):
            kv_ref = kv_refs[n]
            for z in range(0, Z, 2):
                at = n * rows + z * BLK
                keys[at : at + BLK, :] = unpacked_keys(kv_ref.at[z])
                keys[at + BLK : at + 2 * BLK, :] = unpacked_keys(kv_ref.at[z + 1])
                v = jnp.concatenate([kv_ref[z, BLK : 2 * BLK], kv_ref[z + 1, BLK : 2 * BLK]], axis=0)
                values_t[:, at : at + 2 * BLK] = v.T

    q = jnp.concatenate([q_ref[0], q_ref[1]], axis=1)
    width = q.shape[1]
    late = 2 * BLK
    row = lax.broadcasted_iota(jnp.int32, (late, width), 0)
    lane = lax.broadcasted_iota(jnp.int32, (late, width), 1)
    token0 = (Z - 2 + row // BLK) * (X * C * BLK) + row % BLK
    query_pos = base + lane % TILE
    top = jnp.full((1, width), NEGATIVE, jnp.float32)
    for n in range(X):
        s = jnp.dot(keys[n * rows : (n + 1) * rows, :], q, preferred_element_type=jnp.float32)
        token = token0 + ((x + X - n) % X * C + c) * BLK
        tail = jnp.where(token * CSTRIDE + CLEN - 1 <= query_pos, s[rows - late :], NEGATIVE)
        scores[n * rows : (n + 1) * rows - late, :] = s[: rows - late]
        scores[(n + 1) * rows - late : (n + 1) * rows, :] = tail
        top = jnp.maximum(top, jnp.max(s[: rows - late], axis=0, keepdims=True))
        top = jnp.maximum(top, jnp.max(tail, axis=0, keepdims=True))
    total = jnp.zeros((1, width), jnp.float32)
    acc = jnp.zeros((DV, width), jnp.float32)
    for n in range(X):
        w = jnp.exp2((scores[n * rows : (n + 1) * rows, :] - top) * EXP_SCALE)
        total = total + jnp.sum(w, axis=0, keepdims=True)
        acc = acc + jnp.dot(
            values_t[:, n * rows : (n + 1) * rows], w.astype(jnp.bfloat16), preferred_element_type=jnp.float32
        )
    acc = acc * (1.0 / total)
    lse = top * EXP_SCALE + jnp.log(total) * math.log2(math.e)
    for i in range(2):
        out_ref[i] = acc[:, i * TILE : (i + 1) * TILE].astype(out_ref.dtype)
        lse_ref[i] = lse[:, i * TILE : (i + 1) * TILE]


def in_hbm(x):
    return pltpu.with_memory_space_constraint(x, pltpu.HBM)


def coarse_half(info, coarse, queries_t, dtype):
    heads = queries_t.shape[0]
    tokens = X * Z * BLK
    pair = lambda shape: pl.BlockSpec((2, *shape), lambda p, i: (p, 0, 0))
    return pl.pallas_call(
        coarse_kernel,
        grid_spec=pltpu.PrefetchScalarGridSpec(
            num_scalar_prefetch=1,
            grid=(heads // 2,),
            in_specs=[
                *[pl.BlockSpec(a.shape, lambda p, i: (0, 0, 0), pipeline_mode=pl.Buffered(1)) for a in coarse],
                pair((DQK, TILE)),
            ],
            out_specs=[pair((DV, TILE)), pair((1, TILE))],
            scratch_shapes=[
                pltpu.VMEM((tokens, DQK), jnp.bfloat16),
                pltpu.VMEM((DV, tokens), jnp.bfloat16),
                pltpu.VMEM((tokens, 2 * TILE), jnp.float32),
            ],
        ),
        out_shape=[
            jax.ShapeDtypeStruct((heads, DV, TILE), dtype),
            jax.ShapeDtypeStruct((heads, 1, TILE), jnp.float32),
        ],
        cost_estimate=pl.CostEstimate(
            flops=int(EARLY * 2 * heads * TILE) * tokens * (DQK + DV),
            bytes_accessed=tokens * (DQK + DV) * 2 + heads * TILE * (DQK * 2 + DV * 4),
            transcendentals=int(EARLY * heads * TILE * tokens),
        ),
        compiler_params=pltpu.CompilerParams(vmem_limit_bytes=20 << 20),
        name="coarse",
    )(info, *coarse, queries_t)


def tail_kernel(n_grp, info_ref, incoming, q_ref, gate_ref, lse_ref, lse2_ref, coarse_ref, coarse2_ref, weight_ref, *rest):
    outs, scratch = rest[:n_grp], rest[n_grp:]
    queries, coarse, coarse2, weight, keys, values_t, attended, in_sem, weight_sem = scratch
    heads = queries.shape[0]
    cols = weight.shape[1] // n_grp
    base, grp = info_ref[0], info_ref[1]
    q_copy = pltpu.make_async_copy(q_ref, queries, in_sem.at[0])
    coarse_copy = pltpu.make_async_copy(coarse_ref, coarse, in_sem.at[1])
    coarse2_copy = pltpu.make_async_copy(coarse2_ref, coarse2, in_sem.at[2])
    q_copy.start()
    coarse_copy.start()
    coarse2_copy.start()
    late = SEL - 1
    for j in range(SEL):
        late = jnp.where(info_ref[3 + j] * BLK >= base, j, late)
    owners = []
    for j in range(SEL):
        slot_from = jnp.where(late == j, SEL - 1, j) if j < SEL - 1 else late
        owners.append(info_ref[3 + slot_from] >> OWNED_BITS)
    for j in range(0, SEL, 2):
        first, second = incoming.at[owners[j]], incoming.at[owners[j + 1]]
        keys[j * BLK : (j + 1) * BLK, :] = unpacked_keys(first)
        keys[(j + 1) * BLK : (j + 2) * BLK, :] = unpacked_keys(second)
        v = jnp.concatenate([first[BLK : 2 * BLK], second[BLK : 2 * BLK]], axis=0)
        values_t[:, j * BLK : (j + 2) * BLK] = v.T
    q_copy.wait()
    coarse_copy.wait()
    coarse2_copy.wait()
    n_copies = weight_sem.shape[0]
    per_copy = weight.shape[0] // n_copies
    weight_copies = []
    for k in range(n_copies):
        rows = pl.ds(k * per_copy, per_copy)
        weight_copies.append(pltpu.make_async_copy(weight_ref.at[rows], weight.at[rows], weight_sem.at[k]))
    for copy in weight_copies:
        copy.start()
    width = 2 * TILE
    n_keys = SEL * BLK
    row = lax.broadcasted_iota(jnp.int32, (BLK, width), 0)
    lane = lax.broadcasted_iota(jnp.int32, (BLK, width), 1)
    seen = info_ref[3 + late] * BLK + row <= base + lane % TILE

    piece = 2 * BLK
    for p in range(heads // 2):
        q = jnp.concatenate([queries[2 * p], queries[2 * p + 1]], axis=1)
        top = jnp.full((1, width), NEGATIVE, jnp.float32)
        pieces = []
        for at in range(0, n_keys, piece):
            s = jnp.dot(keys[at : at + piece, :], q, preferred_element_type=jnp.float32)
            if at + piece == n_keys:
                s = jnp.concatenate([s[: piece - BLK], jnp.where(seen, s[piece - BLK :], NEGATIVE)], axis=0)
            pieces.append(s)
            top = jnp.maximum(top, jnp.max(s, axis=0, keepdims=True))
        top = top * EXP_SCALE
        total = jnp.zeros((1, width), jnp.float32)
        o = jnp.zeros((DV, width), jnp.float32)
        for n, s in enumerate(pieces):
            w = jnp.exp2(s * EXP_SCALE - top)
            total = total + jnp.sum(w, axis=0, keepdims=True)
            o = o + jnp.dot(
                values_t[:, n * piece : (n + 1) * piece], w.astype(jnp.bfloat16), preferred_element_type=jnp.float32
            )
        gate = jnp.concatenate([gate_ref[heads + 2 * p], gate_ref[heads + 2 * p + 1]], axis=1)
        o = o * (gate / total)
        both = []
        for i in range(2):
            h = 2 * p + i
            gap = lse2_ref[h] - lse_ref[h]
            out = o[:, i * TILE : (i + 1) * TILE] + coarse[h] * (gate_ref[h] / (1.0 + jnp.exp2(gap)))
            out = out + coarse2[h].astype(jnp.float32) * (gate_ref[h] / (1.0 + jnp.exp2(-gap)))
            both.append(out.T.astype(jnp.bfloat16))
        attended[:, 2 * p * DV : 2 * (p + 1) * DV] = jnp.concatenate(both, axis=1)
    for copy in weight_copies:
        copy.wait()
    for k in (*range(1, n_grp), 0):
        at = pl.multiple_of(lax.rem(grp + k, n_grp) * cols, DV)
        part = jnp.dot(attended[...], weight[:, pl.ds(at, cols)], preferred_element_type=jnp.float32)
        outs[k][...] = part.astype(outs[k].dtype)


def tail(info, incoming, queries_t, gate, coarse, coarse2, out_weight, n_grp):
    heads = queries_t.shape[0]
    rows, model = out_weight.shape
    cols = model // n_grp
    vmem = lambda shape: pl.BlockSpec(shape, lambda i, s: (0,) * len(shape))
    on_chip = pl.BlockSpec(memory_space=pltpu.VMEM)
    hbm = pl.BlockSpec(memory_space=pltpu.HBM)
    return pl.pallas_call(
        functools.partial(tail_kernel, n_grp),
        grid_spec=pltpu.PrefetchScalarGridSpec(
            num_scalar_prefetch=1,
            grid=(1,),
            in_specs=[
                on_chip,
                hbm,
                vmem(gate.shape),
                vmem(coarse[1].shape),
                vmem(coarse[1].shape),
                hbm,
                hbm,
                hbm,
            ],
            out_specs=[vmem((TILE, cols))] * n_grp,
            scratch_shapes=[
                pltpu.VMEM(queries_t.shape, queries_t.dtype),
                pltpu.VMEM(coarse[0].shape, coarse[0].dtype),
                pltpu.VMEM(coarse2[0].shape, coarse2[0].dtype),
                pltpu.VMEM((rows, model), jnp.bfloat16),
                pltpu.VMEM((SEL * BLK, DQK), jnp.bfloat16),
                pltpu.VMEM((DV, SEL * BLK), jnp.bfloat16),
                pltpu.VMEM((TILE, rows), jnp.bfloat16),
                pltpu.SemaphoreType.DMA((3,)),
                pltpu.SemaphoreType.DMA((4,)),
            ],
        ),
        out_shape=[jax.ShapeDtypeStruct((TILE, cols), jnp.float32)]
        + [jax.ShapeDtypeStruct((TILE, cols), jnp.bfloat16)] * (n_grp - 1),
        cost_estimate=pl.CostEstimate(
            flops=2 * heads * TILE * SEL * BLK * (DQK + DV) + 2 * TILE * rows * model,
            bytes_accessed=rows * model * 2,
            transcendentals=heads * TILE * SEL * BLK,
        ),
        compiler_params=pltpu.CompilerParams(vmem_limit_bytes=24 << 20),
        name="tail",
    )(
        info,
        incoming,
        in_hbm(queries_t),
        gate,
        coarse[1],
        coarse2[1],
        in_hbm(coarse[0]),
        in_hbm(coarse2[0]),
        in_hbm(out_weight),
    )


def shards(
    queries,
    key_cache,
    group_value_cache,
    coarse_keys,
    coarse_values,
    hidden,
    gate_weight,
    out_weight,
    selected,
):
    seq_count = lax.axis_size("seq")
    n_grp = lax.axis_size("grp")
    seq_index = lax.axis_index("seq")
    grp_index = lax.axis_index("grp")
    ctx_dev = key_cache.shape[1]
    context = ctx_dev * seq_count
    heads = queries.shape[1]
    blocks_dev = ctx_dev // BLK

    own_list = selected[0, 0]
    queries_t = jnp.transpose(queries, (1, 2, 0))
    other_q = shifted(queries_t, 0, 1)

    came = lax.all_to_all(
        letters(own_list, coarse_keys, coarse_values), "seq", 0, 0, axis_index_groups=ALONG_Z, tiled=True
    )
    wanted = jnp.transpose(came[:, PACK, : X * C])[:, None, :].astype(jnp.int32)
    column, wanted, other_q = lax.optimization_barrier((came, wanted, other_q))
    wanted = lax.all_to_all(wanted, "seq", 0, 0, axis_index_groups=IN_PLANE, tiled=True)
    coarse = [column] + [shifted(column, k, 0) for k in range(1, X)]

    blocks = packed_blocks(
        key_cache[0].reshape(blocks_dev, BLK, DQK), group_value_cache[0].reshape(blocks_dev, BLK, DV)
    )
    incoming = lax.all_to_all(payload(wanted, blocks), "seq", 0, 0, tiled=True)

    first_query = context - TILE * seq_count
    x_index, c_index = seq_index // C % X, seq_index % C
    scalars = lambda *values: jnp.stack(values).astype(jnp.int32)
    other_index = seq_index + 1 - 2 * c_index
    gates = jax.nn.sigmoid(
        lax.dot_general(
            gate_weight[0], hidden, (((0,), (1,)), ((), ())), preferred_element_type=jnp.float32
        )
    )[:, None, :]
    first_pos = first_query + seq_index * TILE
    theirs = coarse_half(scalars(first_query + other_index * TILE, x_index, c_index), coarse, other_q, jnp.bfloat16)
    coarse2 = [shifted(a, 0, 1) for a in theirs]
    coarse1 = coarse_half(scalars(first_pos, x_index, c_index), coarse, queries_t, jnp.float32)
    info = jnp.concatenate([scalars(first_pos, grp_index, seq_index), own_list])
    own, *others = tail(info, incoming, queries_t, gates, coarse1, coarse2, out_weight, n_grp)
    for k, part in enumerate(others, 1):
        perm = [(i, (i + k) % n_grp) for i in range(n_grp)]
        own = own + lax.ppermute(part, "grp", perm).astype(jnp.float32)
    return own.astype(jnp.bfloat16)


def solution(mesh):
    return jax.shard_map(
        shards,
        mesh=mesh,
        in_specs=(
            P("seq", "grp", None),
            P("grp", "seq", None),
            P("grp", "seq", None),
            P("grp", "seq", None),
            P("grp", "seq", None),
            P("seq", None),
            P("grp", None, None),
            P("grp", None),
            P("grp", "seq", None),
        ),
        out_specs=P("seq", "grp"),
        check_vma=False,
    )
```

```python
import functools
import math

import jax
import jax.numpy as jnp
from jax import lax
from jax.experimental import pallas as pl
from jax.experimental.pallas import tpu as pltpu
from jax.sharding import PartitionSpec as P

BLK = 64
SEL = 16
TILE = 128
CSTRIDE = 16
CLEN = 32
DQK = 192
DV = 128
PACK = BLK + BLK + BLK // 2
LETTER = PACK + 8
OWNED_BITS = 4
OWNED = 1 << OWNED_BITS
EARLY = 9.62
NEGATIVE = -1e30
EXP_SCALE = DQK**-0.5 * math.log2(math.e)
Z, X, C = 8, 4, 2


def packed_blocks(keys, values):
    high = jnp.concatenate([keys[:, : BLK // 2, DV:], keys[:, BLK // 2 :, DV:]], axis=2)
    return jnp.concatenate([keys[:, :, :DV], values, high], axis=1)


def unpacked_keys(block):
    high = jnp.concatenate([block[2 * BLK : PACK, :BLK], block[2 * BLK : PACK, BLK:]], axis=0)
    return jnp.concatenate([block[:BLK], high], axis=1)


def index(z, x, c):
    return ((z % Z) * X + x % X) * C + c % C


SITES = [(z, x, c) for z in range(Z) for x in range(X) for c in range(C)]
ALONG_Z = [[index(z, x, c) for z in range(Z)] for x in range(X) for c in range(C)]
IN_PLANE = [[index(z, x, c) for x in range(X) for c in range(C)] for z in range(Z)]


def shifted(x, dx, dc):
    return lax.ppermute(x, "seq", [(index(*s), index(s[0], s[1] + dx, s[2] + dc)) for s in SITES])


def letter_kernel(list_ref, keys_ref, values_ref, out_ref):
    keys = keys_ref[0]
    high = jnp.concatenate([keys[: BLK // 2, DV:], keys[BLK // 2 :, DV:]], axis=1)
    lane = lax.broadcasted_iota(jnp.int32, (LETTER - PACK, DV), 1)
    wishes = [(list_ref[j] >> OWNED_BITS, (list_ref[j] & (OWNED - 1)).astype(jnp.float32)) for j in range(SEL)]
    for z in range(Z):
        out_ref[z, :BLK] = keys[:, :DV]
        out_ref[z, BLK : 2 * BLK] = values_ref[0]
        out_ref[z, 2 * BLK : PACK] = high
        wanted = jnp.zeros(lane.shape, jnp.float32)
        for owner, block in wishes:
            wanted = jnp.where(lane == owner - z * (X * C), block, wanted)
        out_ref[z, PACK:] = wanted.astype(jnp.bfloat16)


def letters(own_list, keys, values):
    return pl.pallas_call(
        letter_kernel,
        grid_spec=pltpu.PrefetchScalarGridSpec(
            num_scalar_prefetch=1,
            grid=(1,),
            in_specs=[pl.BlockSpec(a.shape, lambda i, s: (0, 0, 0)) for a in (keys, values)],
            out_specs=pl.BlockSpec((Z, LETTER, DV), lambda i, s: (0, 0, 0)),
        ),
        out_shape=jax.ShapeDtypeStruct((Z, LETTER, DV), keys.dtype),
        cost_estimate=pl.CostEstimate(flops=0, bytes_accessed=Z * LETTER * DV * 2, transcendentals=0),
        name="letters",
    )(own_list, keys, values)


def payload_kernel(wanted_ref, blocks_ref, out_ref):
    z0 = pl.program_id(0) * (out_ref.shape[0] // (X * C))
    for t in range(out_ref.shape[0]):
        z, at = divmod(t, X * C)
        out_ref[t] = blocks_ref[wanted_ref[at, 0, z0 + z]]


def payload(wanted, blocks):
    tiles = wanted.shape[0] * wanted.shape[2]
    steps = 4
    return pl.pallas_call(
        payload_kernel,
        grid_spec=pltpu.PrefetchScalarGridSpec(
            num_scalar_prefetch=1,
            grid=(steps,),
            in_specs=[pl.BlockSpec(blocks.shape, lambda i, w: (0, 0, 0))],
            out_specs=pl.BlockSpec((tiles // steps, PACK, DV), lambda i, w: (i, 0, 0)),
        ),
        out_shape=jax.ShapeDtypeStruct((tiles, PACK, DV), blocks.dtype),
        cost_estimate=pl.CostEstimate(flops=0, bytes_accessed=2 * tiles * PACK * DV * 2, transcendentals=0),
        compiler_params=pltpu.CompilerParams(vmem_limit_bytes=16 << 20),
        name="payload",
    )(wanted, blocks)


def coarse_kernel(info_ref, *rest):
    kv_refs, (q_ref, out_ref, lse_ref, keys, values_t, scores) = rest[:X], rest[X:]
    rows = Z * BLK
    base, x, c = info_ref[0], info_ref[1], info_ref[2]

    @pl.when(pl.program_id(0) == 0)
    def _():
        for n in range(X):
            kv_ref = kv_refs[n]
            for z in range(0, Z, 2):
                at = n * rows + z * BLK
                keys[at : at + BLK, :] = unpacked_keys(kv_ref.at[z])
                keys[at + BLK : at + 2 * BLK, :] = unpacked_keys(kv_ref.at[z + 1])
                v = jnp.concatenate([kv_ref[z, BLK : 2 * BLK], kv_ref[z + 1, BLK : 2 * BLK]], axis=0)
                values_t[:, at : at + 2 * BLK] = v.T

    q = jnp.concatenate([q_ref[0], q_ref[1]], axis=1)
    width = q.shape[1]
    late = 2 * BLK
    row = lax.broadcasted_iota(jnp.int32, (late, width), 0)
    lane = lax.broadcasted_iota(jnp.int32, (late, width), 1)
    token0 = (Z - 2 + row // BLK) * (X * C * BLK) + row % BLK
    query_pos = base + lane % TILE
    top = jnp.full((1, width), NEGATIVE, jnp.float32)
    for n in range(X):
        s = jnp.dot(keys[n * rows : (n + 1) * rows, :], q, preferred_element_type=jnp.float32)
        token = token0 + ((x + X - n) % X * C + c) * BLK
        tail = jnp.where(token * CSTRIDE + CLEN - 1 <= query_pos, s[rows - late :], NEGATIVE)
        scores[n * rows : (n + 1) * rows - late, :] = s[: rows - late]
        scores[(n + 1) * rows - late : (n + 1) * rows, :] = tail
        top = jnp.maximum(top, jnp.max(s[: rows - late], axis=0, keepdims=True))
        top = jnp.maximum(top, jnp.max(tail, axis=0, keepdims=True))
    total = jnp.zeros((1, width), jnp.float32)
    acc = jnp.zeros((DV, width), jnp.float32)
    for n in range(X):
        w = jnp.exp2((scores[n * rows : (n + 1) * rows, :] - top) * EXP_SCALE)
        total = total + jnp.sum(w, axis=0, keepdims=True)
        acc = acc + jnp.dot(
            values_t[:, n * rows : (n + 1) * rows], w.astype(jnp.bfloat16), preferred_element_type=jnp.float32
        )
    acc = acc * (1.0 / total)
    lse = top * EXP_SCALE + jnp.log(total) * math.log2(math.e)
    for i in range(2):
        out_ref[i] = acc[:, i * TILE : (i + 1) * TILE].astype(out_ref.dtype)
        lse_ref[i] = lse[:, i * TILE : (i + 1) * TILE]


def in_hbm(x):
    return pltpu.with_memory_space_constraint(x, pltpu.HBM)


def coarse_half(info, coarse, queries_t, dtype):
    heads = queries_t.shape[0]
    tokens = X * Z * BLK
    pair = lambda shape: pl.BlockSpec((2, *shape), lambda p, i: (p, 0, 0))
    return pl.pallas_call(
        coarse_kernel,
        grid_spec=pltpu.PrefetchScalarGridSpec(
            num_scalar_prefetch=1,
            grid=(heads // 2,),
            in_specs=[
                *[pl.BlockSpec(a.shape, lambda p, i: (0, 0, 0), pipeline_mode=pl.Buffered(1)) for a in coarse],
                pair((DQK, TILE)),
            ],
            out_specs=[pair((DV, TILE)), pair((1, TILE))],
            scratch_shapes=[
                pltpu.VMEM((tokens, DQK), jnp.bfloat16),
                pltpu.VMEM((DV, tokens), jnp.bfloat16),
                pltpu.VMEM((tokens, 2 * TILE), jnp.float32),
            ],
        ),
        out_shape=[
            jax.ShapeDtypeStruct((heads, DV, TILE), dtype),
            jax.ShapeDtypeStruct((heads, 1, TILE), jnp.float32),
        ],
        cost_estimate=pl.CostEstimate(
            flops=int(EARLY * 2 * heads * TILE) * tokens * (DQK + DV),
            bytes_accessed=tokens * (DQK + DV) * 2 + heads * TILE * (DQK * 2 + DV * 4),
            transcendentals=int(EARLY * heads * TILE * tokens),
        ),
        compiler_params=pltpu.CompilerParams(vmem_limit_bytes=20 << 20),
        name="coarse",
    )(info, *coarse, queries_t)


def tail_kernel(n_grp, info_ref, incoming, q_ref, gate_ref, lse_ref, lse2_ref, coarse_ref, coarse2_ref, weight_ref, *rest):
    outs, scratch = rest[:n_grp], rest[n_grp:]
    queries, coarse, coarse2, weight, keys, values_t, attended, in_sem, weight_sem = scratch
    heads = queries.shape[0]
    cols = weight.shape[1] // n_grp
    base, grp = info_ref[0], info_ref[1]
    q_copy = pltpu.make_async_copy(q_ref, queries, in_sem.at[0])
    coarse_copy = pltpu.make_async_copy(coarse_ref, coarse, in_sem.at[1])
    coarse2_copy = pltpu.make_async_copy(coarse2_ref, coarse2, in_sem.at[2])
    q_copy.start()
    coarse_copy.start()
    coarse2_copy.start()
    late = SEL - 1
    for j in range(SEL):
        late = jnp.where(info_ref[3 + j] * BLK >= base, j, late)
    owners = []
    for j in range(SEL):
        slot_from = jnp.where(late == j, SEL - 1, j) if j < SEL - 1 else late
        owners.append(info_ref[3 + slot_from] >> OWNED_BITS)
    for j in range(0, SEL, 2):
        first, second = incoming.at[owners[j]], incoming.at[owners[j + 1]]
        keys[j * BLK : (j + 1) * BLK, :] = unpacked_keys(first)
        keys[(j + 1) * BLK : (j + 2) * BLK, :] = unpacked_keys(second)
        v = jnp.concatenate([first[BLK : 2 * BLK], second[BLK : 2 * BLK]], axis=0)
        values_t[:, j * BLK : (j + 2) * BLK] = v.T
    q_copy.wait()
    coarse_copy.wait()
    coarse2_copy.wait()
    n_copies = weight_sem.shape[0]
    per_copy = weight.shape[0] // n_copies
    weight_copies = []
    for k in range(n_copies):
        rows = pl.ds(k * per_copy, per_copy)
        weight_copies.append(pltpu.make_async_copy(weight_ref.at[rows], weight.at[rows], weight_sem.at[k]))
    for copy in weight_copies:
        copy.start()
    width = 2 * TILE
    n_keys = SEL * BLK
    row = lax.broadcasted_iota(jnp.int32, (BLK, width), 0)
    lane = lax.broadcasted_iota(jnp.int32, (BLK, width), 1)
    seen = info_ref[3 + late] * BLK + row <= base + lane % TILE

    piece = 2 * BLK
    for p in range(heads // 2):
        q = jnp.concatenate([queries[2 * p], queries[2 * p + 1]], axis=1)
        top = jnp.full((1, width), NEGATIVE, jnp.float32)
        pieces = []
        for at in range(0, n_keys, piece):
            s = jnp.dot(keys[at : at + piece, :], q, preferred_element_type=jnp.float32)
            if at + piece == n_keys:
                s = jnp.concatenate([s[: piece - BLK], jnp.where(seen, s[piece - BLK :], NEGATIVE)], axis=0)
            pieces.append(s)
            top = jnp.maximum(top, jnp.max(s, axis=0, keepdims=True))
        top = top * EXP_SCALE
        total = jnp.zeros((1, width), jnp.float32)
        o = jnp.zeros((DV, width), jnp.float32)
        for n, s in enumerate(pieces):
            w = jnp.exp2(s * EXP_SCALE - top)
            total = total + jnp.sum(w, axis=0, keepdims=True)
            o = o + jnp.dot(
                values_t[:, n * piece : (n + 1) * piece], w.astype(jnp.bfloat16), preferred_element_type=jnp.float32
            )
        gate = jnp.concatenate([gate_ref[heads + 2 * p], gate_ref[heads + 2 * p + 1]], axis=1)
        o = o * (gate / total)
        both = []
        for i in range(2):
            h = 2 * p + i
            gap = lse2_ref[h] - lse_ref[h]
            out = o[:, i * TILE : (i + 1) * TILE] + coarse[h] * (gate_ref[h] / (1.0 + jnp.exp2(gap)))
            out = out + coarse2[h].astype(jnp.float32) * (gate_ref[h] / (1.0 + jnp.exp2(-gap)))
            both.append(out.T.astype(jnp.bfloat16))
        attended[:, 2 * p * DV : 2 * (p + 1) * DV] = jnp.concatenate(both, axis=1)
    for copy in weight_copies:
        copy.wait()
    for k in (*range(1, n_grp), 0):
        at = pl.multiple_of(lax.rem(grp + k, n_grp) * cols, DV)
        part = jnp.dot(attended[...], weight[:, pl.ds(at, cols)], preferred_element_type=jnp.float32)
        outs[k][...] = part.astype(outs[k].dtype)


def tail(info, incoming, queries_t, gate, coarse, coarse2, out_weight, n_grp):
    heads = queries_t.shape[0]
    rows, model = out_weight.shape
    cols = model // n_grp
    vmem = lambda shape: pl.BlockSpec(shape, lambda i, s: (0,) * len(shape))
    on_chip = pl.BlockSpec(memory_space=pltpu.VMEM)
    hbm = pl.BlockSpec(memory_space=pltpu.HBM)
    return pl.pallas_call(
        functools.partial(tail_kernel, n_grp),
        grid_spec=pltpu.PrefetchScalarGridSpec(
            num_scalar_prefetch=1,
            grid=(1,),
            in_specs=[
                on_chip,
                hbm,
                vmem(gate.shape),
                vmem(coarse[1].shape),
                vmem(coarse[1].shape),
                hbm,
                hbm,
                hbm,
            ],
            out_specs=[vmem((TILE, cols))] * n_grp,
            scratch_shapes=[
                pltpu.VMEM(queries_t.shape, queries_t.dtype),
                pltpu.VMEM(coarse[0].shape, coarse[0].dtype),
                pltpu.VMEM(coarse2[0].shape, coarse2[0].dtype),
                pltpu.VMEM((rows, model), jnp.bfloat16),
                pltpu.VMEM((SEL * BLK, DQK), jnp.bfloat16),
                pltpu.VMEM((DV, SEL * BLK), jnp.bfloat16),
                pltpu.VMEM((TILE, rows), jnp.bfloat16),
                pltpu.SemaphoreType.DMA((3,)),
                pltpu.SemaphoreType.DMA((4,)),
            ],
        ),
        out_shape=[jax.ShapeDtypeStruct((TILE, cols), jnp.float32)]
        + [jax.ShapeDtypeStruct((TILE, cols), jnp.bfloat16)] * (n_grp - 1),
        cost_estimate=pl.CostEstimate(
            flops=2 * heads * TILE * SEL * BLK * (DQK + DV) + 2 * TILE * rows * model,
            bytes_accessed=rows * model * 2,
            transcendentals=heads * TILE * SEL * BLK,
        ),
        compiler_params=pltpu.CompilerParams(vmem_limit_bytes=24 << 20),
        name="tail",
    )(
        info,
        incoming,
        in_hbm(queries_t),
        gate,
        coarse[1],
        coarse2[1],
        in_hbm(coarse[0]),
        in_hbm(coarse2[0]),
        in_hbm(out_weight),
    )


def shards(
    queries,
    key_cache,
    group_value_cache,
    coarse_keys,
    coarse_values,
    hidden,
    gate_weight,
    out_weight,
    selected,
):
    seq_count = lax.axis_size("seq")
    n_grp = lax.axis_size("grp")
    seq_index = lax.axis_index("seq")
    grp_index = lax.axis_index("grp")
    ctx_dev = key_cache.shape[1]
    context = ctx_dev * seq_count
    heads = queries.shape[1]
    blocks_dev = ctx_dev // BLK

    own_list = selected[0, 0]
    queries_t = jnp.transpose(queries, (1, 2, 0))
    other_q = shifted(queries_t, 0, 1)

    came = lax.all_to_all(
        letters(own_list, coarse_keys, coarse_values), "seq", 0, 0, axis_index_groups=ALONG_Z, tiled=True
    )
    wanted = jnp.transpose(came[:, PACK, : X * C])[:, None, :].astype(jnp.int32)
    column, wanted = lax.optimization_barrier((came, wanted))
    wanted = lax.all_to_all(wanted, "seq", 0, 0, axis_index_groups=IN_PLANE, tiled=True)
    coarse = [column] + [shifted(column, k, 0) for k in range(1, X)]

    blocks = packed_blocks(
        key_cache[0].reshape(blocks_dev, BLK, DQK), group_value_cache[0].reshape(blocks_dev, BLK, DV)
    )
    incoming = lax.all_to_all(payload(wanted, blocks), "seq", 0, 0, tiled=True)

    first_query = context - TILE * seq_count
    x_index, c_index = seq_index // C % X, seq_index % C
    scalars = lambda *values: jnp.stack(values).astype(jnp.int32)
    other_index = seq_index + 1 - 2 * c_index
    gates = jax.nn.sigmoid(
        lax.dot_general(
            gate_weight[0], hidden, (((0,), (1,)), ((), ())), preferred_element_type=jnp.float32
        )
    )[:, None, :]
    first_pos = first_query + seq_index * TILE
    theirs = coarse_half(scalars(first_query + other_index * TILE, x_index, c_index), coarse, other_q, jnp.bfloat16)
    coarse2 = [shifted(a, 0, 1) for a in theirs]
    coarse1 = coarse_half(scalars(first_pos, x_index, c_index), coarse, queries_t, jnp.float32)
    info = jnp.concatenate([scalars(first_pos, grp_index, seq_index), own_list])
    own, *others = tail(info, incoming, queries_t, gates, coarse1, coarse2, out_weight, n_grp)
    for k, part in enumerate(others, 1):
        perm = [(i, (i + k) % n_grp) for i in range(n_grp)]
        own = own + lax.ppermute(part, "grp", perm).astype(jnp.float32)
    return own.astype(jnp.bfloat16)


def solution(mesh):
    return jax.shard_map(
        shards,
        mesh=mesh,
        in_specs=(
            P("seq", "grp", None),
            P("grp", "seq", None),
            P("grp", "seq", None),
            P("grp", "seq", None),
            P("grp", "seq", None),
            P("seq", None),
            P("grp", None, None),
            P("grp", None),
            P("grp", "seq", None),
        ),
        out_specs=P("seq", "grp"),
        check_vma=False,
    )
```

```python
import functools
import math

import jax
import jax.numpy as jnp
from jax import lax
from jax.experimental import pallas as pl
from jax.experimental.pallas import tpu as pltpu
from jax.sharding import PartitionSpec as P

BLK = 64
SEL = 16
TILE = 128
CSTRIDE = 16
CLEN = 32
DQK = 192
DV = 128
PACK = BLK + BLK + BLK // 2
LETTER = PACK + 8
OWNED_BITS = 4
OWNED = 1 << OWNED_BITS
EARLY = 9.62
NEGATIVE = -1e30
EXP_SCALE = DQK**-0.5 * math.log2(math.e)
Z, X, C = 8, 4, 2


def packed_blocks(keys, values):
    high = jnp.concatenate([keys[:, : BLK // 2, DV:], keys[:, BLK // 2 :, DV:]], axis=2)
    return jnp.concatenate([keys[:, :, :DV], values, high], axis=1)


def unpacked_keys(block):
    high = jnp.concatenate([block[2 * BLK : PACK, :BLK], block[2 * BLK : PACK, BLK:]], axis=0)
    return jnp.concatenate([block[:BLK], high], axis=1)


def index(z, x, c):
    return ((z % Z) * X + x % X) * C + c % C


SITES = [(z, x, c) for z in range(Z) for x in range(X) for c in range(C)]
ALONG_Z = [[index(z, x, c) for z in range(Z)] for x in range(X) for c in range(C)]
IN_PLANE = [[index(z, x, c) for x in range(X) for c in range(C)] for z in range(Z)]


def shifted(x, dx, dc):
    return lax.ppermute(x, "seq", [(index(*s), index(s[0], s[1] + dx, s[2] + dc)) for s in SITES])


def letter_kernel(list_ref, keys_ref, values_ref, out_ref):
    keys = keys_ref[0]
    high = jnp.concatenate([keys[: BLK // 2, DV:], keys[BLK // 2 :, DV:]], axis=1)
    lane = lax.broadcasted_iota(jnp.int32, (LETTER - PACK, DV), 1)
    wishes = [(list_ref[j] >> OWNED_BITS, (list_ref[j] & (OWNED - 1)).astype(jnp.float32)) for j in range(SEL)]
    for z in range(Z):
        out_ref[z, :BLK] = keys[:, :DV]
        out_ref[z, BLK : 2 * BLK] = values_ref[0]
        out_ref[z, 2 * BLK : PACK] = high
        wanted = jnp.zeros(lane.shape, jnp.float32)
        for owner, block in wishes:
            wanted = jnp.where(lane == owner - z * (X * C), block, wanted)
        out_ref[z, PACK:] = wanted.astype(jnp.bfloat16)


def letters(own_list, keys, values):
    return pl.pallas_call(
        letter_kernel,
        in_specs=[
            pl.BlockSpec(memory_space=pltpu.SMEM),
            pl.BlockSpec(memory_space=pltpu.VMEM),
            pl.BlockSpec(memory_space=pltpu.VMEM),
        ],
        out_specs=pl.BlockSpec(memory_space=pltpu.VMEM),
        out_shape=jax.ShapeDtypeStruct((Z, LETTER, DV), keys.dtype),
        cost_estimate=pl.CostEstimate(flops=0, bytes_accessed=Z * LETTER * DV * 2, transcendentals=0),
        name="letters",
    )(own_list, keys, values)


def payload_kernel(wanted_ref, blocks_ref, out_ref):
    z0 = pl.program_id(0) * (out_ref.shape[0] // (X * C))
    for t in range(out_ref.shape[0]):
        z, at = divmod(t, X * C)
        out_ref[t] = blocks_ref[wanted_ref[at, 0, z0 + z]]


def payload(wanted, blocks):
    tiles = wanted.shape[0] * wanted.shape[2]
    steps = 4
    return pl.pallas_call(
        payload_kernel,
        grid_spec=pltpu.PrefetchScalarGridSpec(
            num_scalar_prefetch=1,
            grid=(steps,),
            in_specs=[pl.BlockSpec(blocks.shape, lambda i, w: (0, 0, 0))],
            out_specs=pl.BlockSpec((tiles // steps, PACK, DV), lambda i, w: (i, 0, 0)),
        ),
        out_shape=jax.ShapeDtypeStruct((tiles, PACK, DV), blocks.dtype),
        cost_estimate=pl.CostEstimate(flops=0, bytes_accessed=2 * tiles * PACK * DV * 2, transcendentals=0),
        compiler_params=pltpu.CompilerParams(vmem_limit_bytes=16 << 20),
        name="payload",
    )(wanted, blocks)


def coarse_kernel(info_ref, *rest):
    kv_refs, (q_ref, out_ref, lse_ref, keys, values_t, scores) = rest[:X], rest[X:]
    rows = Z * BLK
    base, x, c = info_ref[0], info_ref[1], info_ref[2]

    @pl.when(pl.program_id(0) == 0)
    def _():
        for n in range(X):
            kv_ref = kv_refs[n]
            for z in range(0, Z, 2):
                at = n * rows + z * BLK
                keys[at : at + BLK, :] = unpacked_keys(kv_ref.at[z])
                keys[at + BLK : at + 2 * BLK, :] = unpacked_keys(kv_ref.at[z + 1])
                v = jnp.concatenate([kv_ref[z, BLK : 2 * BLK], kv_ref[z + 1, BLK : 2 * BLK]], axis=0)
                values_t[:, at : at + 2 * BLK] = v.T

    q = jnp.concatenate([q_ref[0], q_ref[1]], axis=1)
    width = q.shape[1]
    late = 2 * BLK
    row = lax.broadcasted_iota(jnp.int32, (late, width), 0)
    lane = lax.broadcasted_iota(jnp.int32, (late, width), 1)
    token0 = (Z - 2 + row // BLK) * (X * C * BLK) + row % BLK
    query_pos = base + lane % TILE
    top = jnp.full((1, width), NEGATIVE, jnp.float32)
    for n in range(X):
        s = jnp.dot(keys[n * rows : (n + 1) * rows, :], q, preferred_element_type=jnp.float32)
        token = token0 + ((x + X - n) % X * C + c) * BLK
        tail = jnp.where(token * CSTRIDE + CLEN - 1 <= query_pos, s[rows - late :], NEGATIVE)
        scores[n * rows : (n + 1) * rows - late, :] = s[: rows - late]
        scores[(n + 1) * rows - late : (n + 1) * rows, :] = tail
        top = jnp.maximum(top, jnp.max(s[: rows - late], axis=0, keepdims=True))
        top = jnp.maximum(top, jnp.max(tail, axis=0, keepdims=True))
    total = jnp.zeros((1, width), jnp.float32)
    acc = jnp.zeros((DV, width), jnp.float32)
    for n in range(X):
        w = jnp.exp2((scores[n * rows : (n + 1) * rows, :] - top) * EXP_SCALE)
        total = total + jnp.sum(w, axis=0, keepdims=True)
        acc = acc + jnp.dot(
            values_t[:, n * rows : (n + 1) * rows], w.astype(jnp.bfloat16), preferred_element_type=jnp.float32
        )
    acc = acc * (1.0 / total)
    lse = top * EXP_SCALE + jnp.log(total) * math.log2(math.e)
    for i in range(2):
        out_ref[i] = acc[:, i * TILE : (i + 1) * TILE].astype(out_ref.dtype)
        lse_ref[i] = lse[:, i * TILE : (i + 1) * TILE]


def in_hbm(x):
    return pltpu.with_memory_space_constraint(x, pltpu.HBM)


def coarse_half(info, coarse, queries_t, dtype):
    heads = queries_t.shape[0]
    tokens = X * Z * BLK
    pair = lambda shape: pl.BlockSpec((2, *shape), lambda p, i: (p, 0, 0))
    return pl.pallas_call(
        coarse_kernel,
        grid_spec=pltpu.PrefetchScalarGridSpec(
            num_scalar_prefetch=1,
            grid=(heads // 2,),
            in_specs=[
                *[pl.BlockSpec(a.shape, lambda p, i: (0, 0, 0), pipeline_mode=pl.Buffered(1)) for a in coarse],
                pair((DQK, TILE)),
            ],
            out_specs=[pair((DV, TILE)), pair((1, TILE))],
            scratch_shapes=[
                pltpu.VMEM((tokens, DQK), jnp.bfloat16),
                pltpu.VMEM((DV, tokens), jnp.bfloat16),
                pltpu.VMEM((tokens, 2 * TILE), jnp.float32),
            ],
        ),
        out_shape=[
            jax.ShapeDtypeStruct((heads, DV, TILE), dtype),
            jax.ShapeDtypeStruct((heads, 1, TILE), jnp.float32),
        ],
        cost_estimate=pl.CostEstimate(
            flops=int(EARLY * 2 * heads * TILE) * tokens * (DQK + DV),
            bytes_accessed=tokens * (DQK + DV) * 2 + heads * TILE * (DQK * 2 + DV * 4),
            transcendentals=int(EARLY * heads * TILE * tokens),
        ),
        compiler_params=pltpu.CompilerParams(vmem_limit_bytes=20 << 20),
        name="coarse",
    )(info, *coarse, queries_t)


def tail_kernel(n_grp, info_ref, incoming, q_ref, gate_ref, lse_ref, lse2_ref, coarse_ref, coarse2_ref, weight_ref, *rest):
    outs, scratch = rest[:n_grp], rest[n_grp:]
    queries, coarse, coarse2, weight, keys, values_t, attended, in_sem, weight_sem = scratch
    heads = queries.shape[0]
    cols = weight.shape[1] // n_grp
    base, grp = info_ref[0], info_ref[1]
    q_copy = pltpu.make_async_copy(q_ref, queries, in_sem.at[0])
    coarse_copy = pltpu.make_async_copy(coarse_ref, coarse, in_sem.at[1])
    coarse2_copy = pltpu.make_async_copy(coarse2_ref, coarse2, in_sem.at[2])
    q_copy.start()
    coarse_copy.start()
    coarse2_copy.start()
    late = SEL - 1
    for j in range(SEL):
        late = jnp.where(info_ref[3 + j] * BLK >= base, j, late)
    owners = []
    for j in range(SEL):
        slot_from = jnp.where(late == j, SEL - 1, j) if j < SEL - 1 else late
        owners.append(info_ref[3 + slot_from] >> OWNED_BITS)
    for j in range(0, SEL, 2):
        first, second = incoming.at[owners[j]], incoming.at[owners[j + 1]]
        keys[j * BLK : (j + 1) * BLK, :] = unpacked_keys(first)
        keys[(j + 1) * BLK : (j + 2) * BLK, :] = unpacked_keys(second)
        v = jnp.concatenate([first[BLK : 2 * BLK], second[BLK : 2 * BLK]], axis=0)
        values_t[:, j * BLK : (j + 2) * BLK] = v.T
    q_copy.wait()
    coarse_copy.wait()
    coarse2_copy.wait()
    n_copies = weight_sem.shape[0]
    per_copy = weight.shape[0] // n_copies
    weight_copies = []
    for k in range(n_copies):
        rows = pl.ds(k * per_copy, per_copy)
        weight_copies.append(pltpu.make_async_copy(weight_ref.at[rows], weight.at[rows], weight_sem.at[k]))
    for copy in weight_copies:
        copy.start()
    width = 2 * TILE
    n_keys = SEL * BLK
    row = lax.broadcasted_iota(jnp.int32, (BLK, width), 0)
    lane = lax.broadcasted_iota(jnp.int32, (BLK, width), 1)
    seen = info_ref[3 + late] * BLK + row <= base + lane % TILE

    piece = 2 * BLK
    for p in range(heads // 2):
        q = jnp.concatenate([queries[2 * p], queries[2 * p + 1]], axis=1)
        top = jnp.full((1, width), NEGATIVE, jnp.float32)
        pieces = []
        for at in range(0, n_keys, piece):
            s = jnp.dot(keys[at : at + piece, :], q, preferred_element_type=jnp.float32)
            if at + piece == n_keys:
                s = jnp.concatenate([s[: piece - BLK], jnp.where(seen, s[piece - BLK :], NEGATIVE)], axis=0)
            pieces.append(s)
            top = jnp.maximum(top, jnp.max(s, axis=0, keepdims=True))
        top = top * EXP_SCALE
        total = jnp.zeros((1, width), jnp.float32)
        o = jnp.zeros((DV, width), jnp.float32)
        for n, s in enumerate(pieces):
            w = jnp.exp2(s * EXP_SCALE - top)
            total = total + jnp.sum(w, axis=0, keepdims=True)
            o = o + jnp.dot(
                values_t[:, n * piece : (n + 1) * piece], w.astype(jnp.bfloat16), preferred_element_type=jnp.float32
            )
        gate = jnp.concatenate([gate_ref[heads + 2 * p], gate_ref[heads + 2 * p + 1]], axis=1)
        o = o * (gate / total)
        both = []
        for i in range(2):
            h = 2 * p + i
            gap = lse2_ref[h] - lse_ref[h]
            out = o[:, i * TILE : (i + 1) * TILE] + coarse[h] * (gate_ref[h] / (1.0 + jnp.exp2(gap)))
            out = out + coarse2[h].astype(jnp.float32) * (gate_ref[h] / (1.0 + jnp.exp2(-gap)))
            both.append(out.T.astype(jnp.bfloat16))
        attended[:, 2 * p * DV : 2 * (p + 1) * DV] = jnp.concatenate(both, axis=1)
    for copy in weight_copies:
        copy.wait()
    for k in (*range(1, n_grp), 0):
        at = pl.multiple_of(lax.rem(grp + k, n_grp) * cols, DV)
        part = jnp.dot(attended[...], weight[:, pl.ds(at, cols)], preferred_element_type=jnp.float32)
        outs[k][...] = part.astype(outs[k].dtype)


def tail(info, incoming, queries_t, gate, coarse, coarse2, out_weight, n_grp):
    heads = queries_t.shape[0]
    rows, model = out_weight.shape
    cols = model // n_grp
    vmem = lambda shape: pl.BlockSpec(shape, lambda i, s: (0,) * len(shape))
    on_chip = pl.BlockSpec(memory_space=pltpu.VMEM)
    hbm = pl.BlockSpec(memory_space=pltpu.HBM)
    return pl.pallas_call(
        functools.partial(tail_kernel, n_grp),
        grid_spec=pltpu.PrefetchScalarGridSpec(
            num_scalar_prefetch=1,
            grid=(1,),
            in_specs=[
                on_chip,
                hbm,
                vmem(gate.shape),
                vmem(coarse[1].shape),
                vmem(coarse[1].shape),
                hbm,
                hbm,
                hbm,
            ],
            out_specs=[vmem((TILE, cols))] * n_grp,
            scratch_shapes=[
                pltpu.VMEM(queries_t.shape, queries_t.dtype),
                pltpu.VMEM(coarse[0].shape, coarse[0].dtype),
                pltpu.VMEM(coarse2[0].shape, coarse2[0].dtype),
                pltpu.VMEM((rows, model), jnp.bfloat16),
                pltpu.VMEM((SEL * BLK, DQK), jnp.bfloat16),
                pltpu.VMEM((DV, SEL * BLK), jnp.bfloat16),
                pltpu.VMEM((TILE, rows), jnp.bfloat16),
                pltpu.SemaphoreType.DMA((3,)),
                pltpu.SemaphoreType.DMA((4,)),
            ],
        ),
        out_shape=[jax.ShapeDtypeStruct((TILE, cols), jnp.float32)]
        + [jax.ShapeDtypeStruct((TILE, cols), jnp.bfloat16)] * (n_grp - 1),
        cost_estimate=pl.CostEstimate(
            flops=2 * heads * TILE * SEL * BLK * (DQK + DV) + 2 * TILE * rows * model,
            bytes_accessed=rows * model * 2,
            transcendentals=heads * TILE * SEL * BLK,
        ),
        compiler_params=pltpu.CompilerParams(vmem_limit_bytes=24 << 20),
        name="tail",
    )(
        info,
        incoming,
        in_hbm(queries_t),
        gate,
        coarse[1],
        coarse2[1],
        in_hbm(coarse[0]),
        in_hbm(coarse2[0]),
        in_hbm(out_weight),
    )


def shards(
    queries,
    key_cache,
    group_value_cache,
    coarse_keys,
    coarse_values,
    hidden,
    gate_weight,
    out_weight,
    selected,
):
    seq_count = lax.axis_size("seq")
    n_grp = lax.axis_size("grp")
    seq_index = lax.axis_index("seq")
    grp_index = lax.axis_index("grp")
    ctx_dev = key_cache.shape[1]
    context = ctx_dev * seq_count
    heads = queries.shape[1]
    blocks_dev = ctx_dev // BLK

    own_list = selected[0, 0]
    queries_t = jnp.transpose(queries, (1, 2, 0))
    other_q = shifted(queries_t, 0, 1)

    came = lax.all_to_all(
        letters(own_list, coarse_keys, coarse_values), "seq", 0, 0, axis_index_groups=ALONG_Z, tiled=True
    )
    wanted = lax.dot_general(
        jnp.eye(X * C, DV, dtype=came.dtype),
        came[:, PACK],
        (((1,), (1,)), ((), ())),
        preferred_element_type=jnp.float32,
    )
    wanted = wanted.astype(jnp.int32)[:, None, :]
    column, wanted = lax.optimization_barrier((came, wanted))
    wanted = lax.all_to_all(wanted, "seq", 0, 0, axis_index_groups=IN_PLANE, tiled=True)
    coarse = [column] + [shifted(column, k, 0) for k in range(1, X)]

    blocks = packed_blocks(
        key_cache[0].reshape(blocks_dev, BLK, DQK), group_value_cache[0].reshape(blocks_dev, BLK, DV)
    )
    incoming = lax.all_to_all(payload(wanted, blocks), "seq", 0, 0, tiled=True)

    first_query = context - TILE * seq_count
    x_index, c_index = seq_index // C % X, seq_index % C
    scalars = lambda *values: jnp.stack(values).astype(jnp.int32)
    other_index = seq_index + 1 - 2 * c_index
    gates = jax.nn.sigmoid(
        lax.dot_general(
            gate_weight[0], hidden, (((0,), (1,)), ((), ())), preferred_element_type=jnp.float32
        )
    )[:, None, :]
    first_pos = first_query + seq_index * TILE
    theirs = coarse_half(scalars(first_query + other_index * TILE, x_index, c_index), coarse, other_q, jnp.bfloat16)
    coarse2 = [shifted(a, 0, 1) for a in theirs]
    coarse1 = coarse_half(scalars(first_pos, x_index, c_index), coarse, queries_t, jnp.float32)
    info = jnp.concatenate([scalars(first_pos, grp_index, seq_index), own_list])
    own, *others = tail(info, incoming, queries_t, gates, coarse1, coarse2, out_weight, n_grp)
    for k, part in enumerate(others, 1):
        perm = [(i, (i + k) % n_grp) for i in range(n_grp)]
        own = own + lax.ppermute(part, "grp", perm).astype(jnp.float32)
    return own.astype(jnp.bfloat16)


def solution(mesh):
    return jax.shard_map(
        shards,
        mesh=mesh,
        in_specs=(
            P("seq", "grp", None),
            P("grp", "seq", None),
            P("grp", "seq", None),
            P("grp", "seq", None),
            P("grp", "seq", None),
            P("seq", None),
            P("grp", None, None),
            P("grp", None),
            P("grp", "seq", None),
        ),
        out_specs=P("seq", "grp"),
        check_vma=False,
    )
```

```python
import functools
import math

import jax
import jax.numpy as jnp
from jax import lax
from jax.experimental import pallas as pl
from jax.experimental.pallas import tpu as pltpu
from jax.sharding import PartitionSpec as P

BLK = 64
SEL = 16
TILE = 128
CSTRIDE = 16
CLEN = 32
DQK = 192
DV = 128
PACK = BLK + BLK + BLK // 2
LETTER = PACK + 8
OWNED_BITS = 4
OWNED = 1 << OWNED_BITS
EARLY = 9.62
NEGATIVE = -1e30
EXP_SCALE = DQK**-0.5 * math.log2(math.e)
Z, X, C = 8, 4, 2


def packed_blocks(keys, values):
    high = jnp.concatenate([keys[:, : BLK // 2, DV:], keys[:, BLK // 2 :, DV:]], axis=2)
    return jnp.concatenate([keys[:, :, :DV], values, high], axis=1)


def unpacked_keys(block):
    high = jnp.concatenate([block[2 * BLK : PACK, :BLK], block[2 * BLK : PACK, BLK:]], axis=0)
    return jnp.concatenate([block[:BLK], high], axis=1)


def index(z, x, c):
    return ((z % Z) * X + x % X) * C + c % C


SITES = [(z, x, c) for z in range(Z) for x in range(X) for c in range(C)]
ALONG_Z = [[index(z, x, c) for z in range(Z)] for x in range(X) for c in range(C)]
IN_PLANE = [[index(z, x, c) for x in range(X) for c in range(C)] for z in range(Z)]


def shifted(x, dx, dc):
    return lax.ppermute(x, "seq", [(index(*s), index(s[0], s[1] + dx, s[2] + dc)) for s in SITES])


def letter_kernel(list_ref, keys_ref, values_ref, out_ref):
    keys = keys_ref[0]
    high = jnp.concatenate([keys[: BLK // 2, DV:], keys[BLK // 2 :, DV:]], axis=1)
    lane = lax.broadcasted_iota(jnp.int32, (LETTER - PACK, DV), 1)
    wishes = [(list_ref[j] >> OWNED_BITS, (list_ref[j] & (OWNED - 1)).astype(jnp.float32)) for j in range(SEL)]
    for z in range(Z):
        out_ref[z, :BLK] = keys[:, :DV]
        out_ref[z, BLK : 2 * BLK] = values_ref[0]
        out_ref[z, 2 * BLK : PACK] = high
        wanted = jnp.zeros(lane.shape, jnp.float32)
        for owner, block in wishes:
            wanted = jnp.where(lane == owner - z * (X * C), block, wanted)
        out_ref[z, PACK:] = wanted.astype(jnp.bfloat16)


def letters(own_list, keys, values):
    return pl.pallas_call(
        letter_kernel,
        in_specs=[
            pl.BlockSpec(memory_space=pltpu.SMEM),
            pl.BlockSpec(memory_space=pltpu.VMEM),
            pl.BlockSpec(memory_space=pltpu.VMEM),
        ],
        out_specs=pl.BlockSpec(memory_space=pltpu.VMEM),
        out_shape=jax.ShapeDtypeStruct((Z, LETTER, DV), keys.dtype),
        cost_estimate=pl.CostEstimate(flops=0, bytes_accessed=Z * LETTER * DV * 2, transcendentals=0),
        name="letters",
    )(own_list, keys, values)


def payload_kernel(wanted_ref, blocks_ref, out_ref):
    z0 = pl.program_id(0) * (out_ref.shape[0] // (X * C))
    for t in range(out_ref.shape[0]):
        z, at = divmod(t, X * C)
        out_ref[t] = blocks_ref[wanted_ref[at, 0, z0 + z]]


def payload(wanted, blocks):
    tiles = wanted.shape[0] * wanted.shape[2]
    steps = 4
    return pl.pallas_call(
        payload_kernel,
        grid=(steps,),
        in_specs=[pl.BlockSpec(memory_space=pltpu.SMEM), pl.BlockSpec(blocks.shape, lambda i: (0, 0, 0))],
        out_specs=pl.BlockSpec((tiles // steps, PACK, DV), lambda i: (i, 0, 0)),
        out_shape=jax.ShapeDtypeStruct((tiles, PACK, DV), blocks.dtype),
        cost_estimate=pl.CostEstimate(flops=0, bytes_accessed=2 * tiles * PACK * DV * 2, transcendentals=0),
        compiler_params=pltpu.CompilerParams(vmem_limit_bytes=16 << 20),
        name="payload",
    )(wanted, blocks)


def coarse_kernel(info_ref, *rest):
    kv_refs, (q_ref, out_ref, lse_ref, keys, values_t, scores) = rest[:X], rest[X:]
    rows = Z * BLK
    base, x, c = info_ref[0], info_ref[1], info_ref[2]

    @pl.when(pl.program_id(0) == 0)
    def _():
        for n in range(X):
            kv_ref = kv_refs[n]
            for z in range(0, Z, 2):
                at = n * rows + z * BLK
                keys[at : at + BLK, :] = unpacked_keys(kv_ref.at[z])
                keys[at + BLK : at + 2 * BLK, :] = unpacked_keys(kv_ref.at[z + 1])
                v = jnp.concatenate([kv_ref[z, BLK : 2 * BLK], kv_ref[z + 1, BLK : 2 * BLK]], axis=0)
                values_t[:, at : at + 2 * BLK] = v.T

    q = jnp.concatenate([q_ref[0], q_ref[1]], axis=1)
    width = q.shape[1]
    late = 2 * BLK
    row = lax.broadcasted_iota(jnp.int32, (late, width), 0)
    lane = lax.broadcasted_iota(jnp.int32, (late, width), 1)
    token0 = (Z - 2 + row // BLK) * (X * C * BLK) + row % BLK
    query_pos = base + lane % TILE
    top = jnp.full((1, width), NEGATIVE, jnp.float32)
    for n in range(X):
        s = jnp.dot(keys[n * rows : (n + 1) * rows, :], q, preferred_element_type=jnp.float32)
        token = token0 + ((x + X - n) % X * C + c) * BLK
        tail = jnp.where(token * CSTRIDE + CLEN - 1 <= query_pos, s[rows - late :], NEGATIVE)
        scores[n * rows : (n + 1) * rows - late, :] = s[: rows - late]
        scores[(n + 1) * rows - late : (n + 1) * rows, :] = tail
        top = jnp.maximum(top, jnp.max(s[: rows - late], axis=0, keepdims=True))
        top = jnp.maximum(top, jnp.max(tail, axis=0, keepdims=True))
    total = jnp.zeros((1, width), jnp.float32)
    acc = jnp.zeros((DV, width), jnp.float32)
    for n in range(X):
        w = jnp.exp2((scores[n * rows : (n + 1) * rows, :] - top) * EXP_SCALE)
        total = total + jnp.sum(w, axis=0, keepdims=True)
        acc = acc + jnp.dot(
            values_t[:, n * rows : (n + 1) * rows], w.astype(jnp.bfloat16), preferred_element_type=jnp.float32
        )
    acc = acc * (1.0 / total)
    lse = top * EXP_SCALE + jnp.log(total) * math.log2(math.e)
    for i in range(2):
        out_ref[i] = acc[:, i * TILE : (i + 1) * TILE].astype(out_ref.dtype)
        lse_ref[i] = lse[:, i * TILE : (i + 1) * TILE]


def in_hbm(x):
    return pltpu.with_memory_space_constraint(x, pltpu.HBM)


def coarse_half(info, coarse, queries_t, dtype):
    heads = queries_t.shape[0]
    tokens = X * Z * BLK
    pair = lambda shape: pl.BlockSpec((2, *shape), lambda p, i: (p, 0, 0))
    return pl.pallas_call(
        coarse_kernel,
        grid_spec=pltpu.PrefetchScalarGridSpec(
            num_scalar_prefetch=1,
            grid=(heads // 2,),
            in_specs=[
                *[pl.BlockSpec(a.shape, lambda p, i: (0, 0, 0), pipeline_mode=pl.Buffered(1)) for a in coarse],
                pair((DQK, TILE)),
            ],
            out_specs=[pair((DV, TILE)), pair((1, TILE))],
            scratch_shapes=[
                pltpu.VMEM((tokens, DQK), jnp.bfloat16),
                pltpu.VMEM((DV, tokens), jnp.bfloat16),
                pltpu.VMEM((tokens, 2 * TILE), jnp.float32),
            ],
        ),
        out_shape=[
            jax.ShapeDtypeStruct((heads, DV, TILE), dtype),
            jax.ShapeDtypeStruct((heads, 1, TILE), jnp.float32),
        ],
        cost_estimate=pl.CostEstimate(
            flops=int(EARLY * 2 * heads * TILE) * tokens * (DQK + DV),
            bytes_accessed=tokens * (DQK + DV) * 2 + heads * TILE * (DQK * 2 + DV * 4),
            transcendentals=int(EARLY * heads * TILE * tokens),
        ),
        compiler_params=pltpu.CompilerParams(vmem_limit_bytes=20 << 20),
        name="coarse",
    )(info, *coarse, queries_t)


def tail_kernel(n_grp, info_ref, incoming, q_ref, gate_ref, lse_ref, lse2_ref, coarse_ref, coarse2_ref, weight_ref, *rest):
    outs, scratch = rest[:n_grp], rest[n_grp:]
    queries, coarse, coarse2, weight, keys, values_t, attended, in_sem, weight_sem = scratch
    heads = queries.shape[0]
    cols = weight.shape[1] // n_grp
    base, grp = info_ref[0], info_ref[1]
    q_copy = pltpu.make_async_copy(q_ref, queries, in_sem.at[0])
    coarse_copy = pltpu.make_async_copy(coarse_ref, coarse, in_sem.at[1])
    coarse2_copy = pltpu.make_async_copy(coarse2_ref, coarse2, in_sem.at[2])
    q_copy.start()
    coarse_copy.start()
    coarse2_copy.start()
    late = SEL - 1
    for j in range(SEL):
        late = jnp.where(info_ref[3 + j] * BLK >= base, j, late)
    owners = []
    for j in range(SEL):
        slot_from = jnp.where(late == j, SEL - 1, j) if j < SEL - 1 else late
        owners.append(info_ref[3 + slot_from] >> OWNED_BITS)
    for j in range(0, SEL, 2):
        first, second = incoming.at[owners[j]], incoming.at[owners[j + 1]]
        keys[j * BLK : (j + 1) * BLK, :] = unpacked_keys(first)
        keys[(j + 1) * BLK : (j + 2) * BLK, :] = unpacked_keys(second)
        v = jnp.concatenate([first[BLK : 2 * BLK], second[BLK : 2 * BLK]], axis=0)
        values_t[:, j * BLK : (j + 2) * BLK] = v.T
    q_copy.wait()
    coarse_copy.wait()
    coarse2_copy.wait()
    n_copies = weight_sem.shape[0]
    per_copy = weight.shape[0] // n_copies
    weight_copies = []
    for k in range(n_copies):
        rows = pl.ds(k * per_copy, per_copy)
        weight_copies.append(pltpu.make_async_copy(weight_ref.at[rows], weight.at[rows], weight_sem.at[k]))
    for copy in weight_copies:
        copy.start()
    width = 2 * TILE
    n_keys = SEL * BLK
    row = lax.broadcasted_iota(jnp.int32, (BLK, width), 0)
    lane = lax.broadcasted_iota(jnp.int32, (BLK, width), 1)
    seen = info_ref[3 + late] * BLK + row <= base + lane % TILE

    piece = 2 * BLK
    for p in range(heads // 2):
        q = jnp.concatenate([queries[2 * p], queries[2 * p + 1]], axis=1)
        top = jnp.full((1, width), NEGATIVE, jnp.float32)
        pieces = []
        for at in range(0, n_keys, piece):
            s = jnp.dot(keys[at : at + piece, :], q, preferred_element_type=jnp.float32)
            if at + piece == n_keys:
                s = jnp.concatenate([s[: piece - BLK], jnp.where(seen, s[piece - BLK :], NEGATIVE)], axis=0)
            pieces.append(s)
            top = jnp.maximum(top, jnp.max(s, axis=0, keepdims=True))
        top = top * EXP_SCALE
        total = jnp.zeros((1, width), jnp.float32)
        o = jnp.zeros((DV, width), jnp.float32)
        for n, s in enumerate(pieces):
            w = jnp.exp2(s * EXP_SCALE - top)
            total = total + jnp.sum(w, axis=0, keepdims=True)
            o = o + jnp.dot(
                values_t[:, n * piece : (n + 1) * piece], w.astype(jnp.bfloat16), preferred_element_type=jnp.float32
            )
        gate = jnp.concatenate([gate_ref[heads + 2 * p], gate_ref[heads + 2 * p + 1]], axis=1)
        o = o * (gate / total)
        both = []
        for i in range(2):
            h = 2 * p + i
            gap = lse2_ref[h] - lse_ref[h]
            out = o[:, i * TILE : (i + 1) * TILE] + coarse[h] * (gate_ref[h] / (1.0 + jnp.exp2(gap)))
            out = out + coarse2[h].astype(jnp.float32) * (gate_ref[h] / (1.0 + jnp.exp2(-gap)))
            both.append(out.T.astype(jnp.bfloat16))
        attended[:, 2 * p * DV : 2 * (p + 1) * DV] = jnp.concatenate(both, axis=1)
    for copy in weight_copies:
        copy.wait()
    for k in (*range(1, n_grp), 0):
        at = pl.multiple_of(lax.rem(grp + k, n_grp) * cols, DV)
        part = jnp.dot(attended[...], weight[:, pl.ds(at, cols)], preferred_element_type=jnp.float32)
        outs[k][...] = part.astype(outs[k].dtype)


def tail(info, incoming, queries_t, gate, coarse, coarse2, out_weight, n_grp):
    heads = queries_t.shape[0]
    rows, model = out_weight.shape
    cols = model // n_grp
    vmem = lambda shape: pl.BlockSpec(shape, lambda i, s: (0,) * len(shape))
    on_chip = pl.BlockSpec(memory_space=pltpu.VMEM)
    hbm = pl.BlockSpec(memory_space=pltpu.HBM)
    return pl.pallas_call(
        functools.partial(tail_kernel, n_grp),
        grid_spec=pltpu.PrefetchScalarGridSpec(
            num_scalar_prefetch=1,
            grid=(1,),
            in_specs=[
                on_chip,
                hbm,
                vmem(gate.shape),
                vmem(coarse[1].shape),
                vmem(coarse[1].shape),
                hbm,
                hbm,
                hbm,
            ],
            out_specs=[vmem((TILE, cols))] * n_grp,
            scratch_shapes=[
                pltpu.VMEM(queries_t.shape, queries_t.dtype),
                pltpu.VMEM(coarse[0].shape, coarse[0].dtype),
                pltpu.VMEM(coarse2[0].shape, coarse2[0].dtype),
                pltpu.VMEM((rows, model), jnp.bfloat16),
                pltpu.VMEM((SEL * BLK, DQK), jnp.bfloat16),
                pltpu.VMEM((DV, SEL * BLK), jnp.bfloat16),
                pltpu.VMEM((TILE, rows), jnp.bfloat16),
                pltpu.SemaphoreType.DMA((3,)),
                pltpu.SemaphoreType.DMA((4,)),
            ],
        ),
        out_shape=[jax.ShapeDtypeStruct((TILE, cols), jnp.float32)]
        + [jax.ShapeDtypeStruct((TILE, cols), jnp.bfloat16)] * (n_grp - 1),
        cost_estimate=pl.CostEstimate(
            flops=2 * heads * TILE * SEL * BLK * (DQK + DV) + 2 * TILE * rows * model,
            bytes_accessed=rows * model * 2,
            transcendentals=heads * TILE * SEL * BLK,
        ),
        compiler_params=pltpu.CompilerParams(vmem_limit_bytes=24 << 20),
        name="tail",
    )(
        info,
        incoming,
        in_hbm(queries_t),
        gate,
        coarse[1],
        coarse2[1],
        in_hbm(coarse[0]),
        in_hbm(coarse2[0]),
        in_hbm(out_weight),
    )


def shards(
    queries,
    key_cache,
    group_value_cache,
    coarse_keys,
    coarse_values,
    hidden,
    gate_weight,
    out_weight,
    selected,
):
    seq_count = lax.axis_size("seq")
    n_grp = lax.axis_size("grp")
    seq_index = lax.axis_index("seq")
    grp_index = lax.axis_index("grp")
    ctx_dev = key_cache.shape[1]
    context = ctx_dev * seq_count
    heads = queries.shape[1]
    blocks_dev = ctx_dev // BLK

    own_list = selected[0, 0]
    queries_t = jnp.transpose(queries, (1, 2, 0))
    other_q = shifted(queries_t, 0, 1)

    came = lax.all_to_all(
        letters(own_list, coarse_keys, coarse_values), "seq", 0, 0, axis_index_groups=ALONG_Z, tiled=True
    )
    wanted = lax.dot_general(
        jnp.eye(X * C, DV, dtype=came.dtype),
        came[:, PACK],
        (((1,), (1,)), ((), ())),
        preferred_element_type=jnp.float32,
    )
    wanted = wanted.astype(jnp.int32)[:, None, :]
    column, wanted = lax.optimization_barrier((came, wanted))
    wanted = lax.all_to_all(wanted, "seq", 0, 0, axis_index_groups=IN_PLANE, tiled=True)
    coarse = [column] + [shifted(column, k, 0) for k in range(1, X)]

    blocks = packed_blocks(
        key_cache[0].reshape(blocks_dev, BLK, DQK), group_value_cache[0].reshape(blocks_dev, BLK, DV)
    )
    incoming = lax.all_to_all(payload(wanted, blocks), "seq", 0, 0, tiled=True)

    first_query = context - TILE * seq_count
    x_index, c_index = seq_index // C % X, seq_index % C
    scalars = lambda *values: jnp.stack(values).astype(jnp.int32)
    other_index = seq_index + 1 - 2 * c_index
    gates = jax.nn.sigmoid(
        lax.dot_general(
            gate_weight[0], hidden, (((0,), (1,)), ((), ())), preferred_element_type=jnp.float32
        )
    )[:, None, :]
    first_pos = first_query + seq_index * TILE
    theirs = coarse_half(scalars(first_query + other_index * TILE, x_index, c_index), coarse, other_q, jnp.bfloat16)
    coarse2 = [shifted(a, 0, 1) for a in theirs]
    coarse1 = coarse_half(scalars(first_pos, x_index, c_index), coarse, queries_t, jnp.float32)
    info = jnp.concatenate([scalars(first_pos, grp_index, seq_index), own_list])
    own, *others = tail(info, incoming, queries_t, gates, coarse1, coarse2, out_weight, n_grp)
    for k, part in enumerate(others, 1):
        perm = [(i, (i + k) % n_grp) for i in range(n_grp)]
        own = own + lax.ppermute(part, "grp", perm).astype(jnp.float32)
    return own.astype(jnp.bfloat16)


def solution(mesh):
    return jax.shard_map(
        shards,
        mesh=mesh,
        in_specs=(
            P("seq", "grp", None),
            P("grp", "seq", None),
            P("grp", "seq", None),
            P("grp", "seq", None),
            P("grp", "seq", None),
            P("seq", None),
            P("grp", None, None),
            P("grp", None),
            P("grp", "seq", None),
        ),
        out_specs=P("seq", "grp"),
        check_vma=False,
    )
```
